128 devices in a mesh: blk: 8 (over z_lo, y), inner: 16 (over x, z_hi, core).
Axes of the slice: x: 4, y: 4, z: 4 (z_hi: 2, z_lo: 2; z = z_hi * 2 + z_lo), core: 2. Of those that a mesh axis runs over, the one named last changes fastest.
Arguments:
- queries: bfloat16 [16384, 768], P(('blk', 'inner')), may hold values from -16 to 16
- keys: bfloat16 [16384, 768], P(('blk', 'inner')), may hold values from -16 to 16
- values: bfloat16 [16384, 768], P(('blk', 'inner')), may hold values from -6 to 6
- valid: int32 [16384], P(('blk', 'inner')), may hold values 0 or 1
- out_weight: bfloat16 [768, 768], replicated, may hold values from -0.21875 to 0.21875
Outputs:
- mixed: bfloat16 [16384, 768], P(('blk', 'inner'))
The draws below stay inside these ranges and needn't reach their ends.
All inputs are finite; a program needn't handle non-finite values. No bound on the sum of `valid` on one device may be relied on, other than what follows from the above.
Results may differ from the reference program's by a relative error of at most 0.015.
Values may be sent and summed in bfloat16 or wider, within the bound.
A program may use at most 128 MiB of HBM per device.

```python
import jax
import jax.numpy as jnp
from jax import lax

HEADS = 12
HEAD_DIM = 64
D = 768
TOKENS = 16384


def draw_queries(key, part):
    subkey = jax.random.fold_in(key, 1)
    drawn = jnp.clip(jax.random.normal(subkey, (TOKENS, D), jnp.float32), -8.0, 8.0)
    return drawn.astype(jnp.bfloat16)


def draw_keys(key, part):
    subkey = jax.random.fold_in(key, 2)
    drawn = jnp.clip(jax.random.normal(subkey, (TOKENS, D), jnp.float32), -8.0, 8.0)
    return drawn.astype(jnp.bfloat16)


def place_ends(values, own_key, least, top_value):
    shape = values.shape
    index_at = [jax.random.randint(jax.random.fold_in(own_key, axis), (), 0, shape[axis]) for axis in range(len(shape))]
    values = values.at[tuple(index_at)].set(least)
    longest = shape.index(max(shape))
    index_at[longest] = (index_at[longest] + 1) % shape[longest]
    return values.at[tuple(index_at)].set(top_value)


def levels(key, extent, pieces, least, high):
    def one(dim, parts):
        draws = jax.random.uniform(jax.random.fold_in(jax.random.fold_in(key, 6), dim), (parts,), jnp.float32, least / len(pieces), high / len(pieces))
        return jnp.repeat(jnp.exp(draws), extent[dim] // parts).reshape((-1,) + (1,) * (len(extent) - dim - 1))

    loudness = one(*pieces[0])
    for cut in pieces[1:]:
        loudness = loudness * one(*cut)
    return loudness


def centred(stream_key, extent, spread, most, pieces=(), kind=jnp.bfloat16):
    values = spread * jax.random.normal(stream_key, extent, jnp.float32)
    if pieces:
        values = values * levels(stream_key, extent, pieces, -0.22, 0.18)
    return jnp.clip(values, -most, most).astype(kind)


def setup_inputs(seed: int = 0) -> dict:
    seeds = jax.random.split(jax.random.key(seed), 6)
    queries = draw_queries(jax.random.fold_in(seeds[5], 71), 0)
    keys = draw_keys(jax.random.fold_in(seeds[5], 71), 0)
    values = centred(seeds[2], (TOKENS, D), 1.0, 6.0, ((0, 128),))
    valid = place_ends((jax.random.randint(seeds[3], (TOKENS,), 0, 4) < 3).astype(jnp.int32), jax.random.fold_in(seeds[3], 1), 0, 1)
    out_weight = centred(seeds[4], (D, D), D ** -0.5, 0.21875)
    return dict(queries=queries, keys=keys, values=values, valid=valid, out_weight=out_weight)


def reference(queries, keys, values, valid, out_weight):
    score_scale = HEAD_DIM ** -0.5
    key_heads = keys.astype(jnp.float32).reshape(TOKENS, HEADS, HEAD_DIM)
    value_heads = values.astype(jnp.float32).reshape(TOKENS, HEADS, HEAD_DIM)
    usable = valid > 0
    block_rows = min(512, TOKENS)

    def attend_block(query_block):
        query_heads = query_block.astype(jnp.float32).reshape(block_rows, HEADS, HEAD_DIM)
        scores = jnp.einsum("qhd,khd->hqk", query_heads, key_heads) * score_scale
        scores = jnp.where(usable[None, None, :], scores, -1e30)
        row_top = jnp.maximum(jnp.max(scores, axis=-1), 0.0)
        chances = jnp.exp(scores - row_top[..., None]).astype(jnp.bfloat16)
        chances = lax.optimization_barrier(chances).astype(jnp.float32)
        denominator = jnp.exp(-row_top) + jnp.sum(chances, axis=-1)
        numerator = jnp.einsum("hqk,khd->qhd", chances, value_heads)
        result = numerator / jnp.transpose(denominator)[..., None]
        return result.reshape(block_rows, HEADS * HEAD_DIM).astype(jnp.bfloat16)

    attended = lax.map(attend_block, queries.reshape(TOKENS // block_rows, block_rows, HEADS * HEAD_DIM))
    attended = attended.reshape(TOKENS, HEADS * HEAD_DIM)
    return jnp.dot(attended, out_weight, preferred_element_type=jnp.float32).astype(jnp.bfloat16)
```

```python
import jax
import jax.numpy as jnp
from jax import lax
from jax.experimental import pallas as pl
from jax.experimental.pallas import tpu as pltpu
from jax.sharding import PartitionSpec as P

HEADS = 12
HEAD_DIM = 64
GROUPS = 4
GH = HEADS // GROUPS
ROWS = 128
GD = GH * HEAD_DIM
TILE = 4 * ROWS
KROWS = 2 * ROWS
SHARD = KROWS + GD + 16
LOG2E = 1.4426950408889634
MESH = pl.DeviceIdType.MESH

KA, QA, KX, KS, QY, OY, SY, OZ = 0, 4, 8, 12, 16, 20, 24, 28


def kernel(
    kv_src, q_src, w_ref, out_ref,
    kv, qb, qs, q2, sb, acc, top, shrink, o_send, s_send, o_recv, s_recv, a_send, att,
    send_sem, recv_sem,
):
    blk = lax.axis_index("blk")
    inner = lax.axis_index("inner")
    y, x, c = blk % 4, inner // 4, inner % 2
    z = (inner // 2 % 2) * 2 + blk // 4

    def at(dx=0, dy=0, dz=0, dc=0):
        tx, ty, tz, tc = (x + dx) % 4, (y + dy) % 4, (z + dz) % 4, (c + dc) % 2
        return ((tz % 2) * 4 + ty, tx * 4 + (tz // 2) * 2 + tc)

    def send(src, dst, number, device):
        return pltpu.make_async_remote_copy(
            src_ref=src, dst_ref=dst, send_sem=send_sem.at[number], recv_sem=recv_sem.at[number],
            device_id=device, device_id_type=MESH,
        )

    def keys_z(r):
        return send(kv_src.at[(z + r) % 4], kv.at[0, 0, r], KA + r, at(dz=r))

    def queries_z(r):
        return send(q_src.at[(z + r) % 4], qb.at[0, r], QA + r, at(dz=r))

    def keys_x(r):
        return send(kv.at[0, 0], kv.at[0, r], KX + r, at(dx=r))

    def keys_core(r):
        return send(kv.at[0, r], kv.at[1, r], KS + r, at(dc=1))

    def queries_y(r):
        return send(qb.at[0], qb.at[r], QY + r, at(dy=r))

    def parts_y(r):
        return send(o_send.at[r], o_recv.at[r], OY + r, at(dy=4 - r))

    def stats_y(r):
        return send(s_send.at[r], s_recv.at[r], SY + r, at(dy=4 - r))

    def attended_z(r):
        return send(a_send.at[r], att.at[z], OZ + r, at(dz=4 - r))

    barrier = pltpu.get_barrier_semaphore()
    partners = [at(dc=1)]
    for r in (1, 2, 3):
        partners += [at(dx=r), at(dy=r), at(dz=r)]
    for device in partners:
        pl.semaphore_signal(barrier, inc=1, device_id=device, device_id_type=MESH)
    pl.semaphore_wait(barrier, len(partners))

    for r in (1, 3, 2):
        queries_z(r).start()
    for r in (1, 3, 2):
        keys_z(r).start()
    qb[0, 0] = q_src[z]
    kv[0, 0, 0] = kv_src[z]
    qs[...] = jnp.zeros_like(qs)
    acc[...] = jnp.zeros_like(acc)
    top[...] = jnp.zeros_like(top)

    def prepare(ry):
        for rz in range(4):
            columns = pl.ds(ry * TILE + rz * ROWS, ROWS)
            scaled = qb[ry, rz].astype(jnp.float32) * (LOG2E * HEAD_DIM**-0.5)
            high = scaled.astype(jnp.bfloat16)
            low = (scaled - high.astype(jnp.float32)).astype(jnp.bfloat16)
            for h in range(2):
                rows = slice(h * HEAD_DIM, (h + 1) * HEAD_DIM)
                qs[h, h * HEAD_DIM : (h + 1) * HEAD_DIM, columns] = high[rows]
                qs[h, ROWS + h * HEAD_DIM : ROWS + (h + 1) * HEAD_DIM, columns] = low[rows]
            q2[:HEAD_DIM, columns] = high[2 * HEAD_DIM :]
            q2[HEAD_DIM:, columns] = low[2 * HEAD_DIM :]

    for r in (1, 3, 2):
        queries_z(r).wait_recv()
    for r in (1, 3, 2):
        queries_y(r).start()
    for r in (1, 3, 2):
        keys_z(r).wait_recv()
    keys_core(0).start()
    for r in (1, 3, 2):
        keys_x(r).start()
    prepare(0)
    keys_core(0).wait_recv()

    def gray(p):
        return p + (p // 2) * (1 - 2 * (p % 2))

    def place(g):
        t, p = g // 4, g % 4
        rx = gray(t)
        ry = gray(p + (t // 3) * (3 - 2 * p))
        return rx, ry

    def score(g, h):
        rx, ry = place(g)
        columns = pl.ds(pl.multiple_of(ry * TILE, TILE), TILE)
        first = 0 if h < 2 else ROWS
        keys = jnp.concatenate(
            [kv[cc, rx, rz, first : first + ROWS, :] for cc in range(2) for rz in range(4)], axis=0
        )
        if h < 2:
            keys = jnp.concatenate([keys, keys], axis=1)
            query = qs[h, :, columns]
        else:
            query = q2[:, columns]
        s = jnp.dot(keys, query, preferred_element_type=jnp.float32)
        sb[h] = s
        old = top[h, :, columns]
        new = jnp.maximum(old, jnp.max(s, axis=0, keepdims=True))
        shrink[h] = jnp.exp2(old - new)
        top[h, :, columns] = new

    def weigh(g, h):
        rx, ry = place(g)
        columns = pl.ds(pl.multiple_of(ry * TILE, TILE), TILE)
        chances = jnp.exp2(sb[h] - top[h, :, columns]).astype(jnp.bfloat16)
        first = KROWS + h * HEAD_DIM
        values = jnp.concatenate(
            [
                jnp.concatenate(
                    [kv[cc, rx, rz, first : first + HEAD_DIM, :], kv[cc, rx, rz, KROWS + GD :, :]],
                    axis=0,
                )
                for cc in range(2)
                for rz in range(4)
            ],
            axis=1,
        )
        acc[h, :, columns] = acc[h, :, columns] * shrink[h] + jnp.dot(
            values, chances, preferred_element_type=jnp.float32
        )

    score(0, 0)

    def step(g, carry):
        for n, r in ((1, 1), (2, 3), (3, 2)):

            @pl.when(g == n - 1)
            def _():
                queries_y(r).wait_recv()
                prepare(r)

        for n, r in ((4, 1), (8, 3), (12, 2)):

            @pl.when(g == n - 1)
            def _():
                keys_x(r).wait_recv()
                keys_core(r).start()
                keys_core(r).wait_recv()

        score(g, 1)
        weigh(g, 0)
        score(g, 2)
        weigh(g, 1)
        score(jnp.minimum(g + 1, 15), 0)
        weigh(g, 2)

        for n, r in ((12, 2), (13, 3), (14, 1), (15, 0)):

            @pl.when(g == n)
            def _():
                columns = pl.ds(r * TILE, TILE)
                o_to, s_to = (o_send, s_send) if r else (o_recv, s_recv)
                for h in range(GH):
                    o_to[r, h * HEAD_DIM : (h + 1) * HEAD_DIM, :] = acc[
                        h, :HEAD_DIM, columns
                    ].astype(jnp.bfloat16)
                    s_to[r, h : h + 1, :] = top[h, :, columns]
                    s_to[r, GH + h : GH + h + 1, :] = acc[h, HEAD_DIM : HEAD_DIM + 1, columns]
                s_to[r, 2 * GH :, :] = jnp.zeros((8 - 2 * GH, TILE), jnp.float32)
                if r:
                    stats_y(r).start()
                    parts_y(r).start()

        return carry

    lax.fori_loop(0, 16, step, 0)

    for r in (2, 3, 1):
        stats_y(r).wait_recv()
        parts_y(r).wait_recv()
    for h in range(GH):
        rows = slice(h * HEAD_DIM, (h + 1) * HEAD_DIM)
        tops = [s_recv[r, h : h + 1, :] for r in range(4)]
        most = jnp.maximum(jnp.maximum(tops[0], tops[1]), jnp.maximum(tops[2], tops[3]))
        total = jnp.exp2(-most)
        weighted = jnp.zeros((HEAD_DIM, TILE), jnp.float32)
        for r in range(4):
            factor = jnp.exp2(tops[r] - most)
            total = total + s_recv[r, GH + h : GH + h + 1, :] * factor
            weighted = weighted + o_recv[r, rows, :].astype(jnp.float32) * factor
        done = (weighted / total).astype(jnp.bfloat16)
        for rz in range(4):
            a_send[rz, rows, :] = done[:, rz * ROWS : (rz + 1) * ROWS]
    for r in (1, 3, 2):
        attended_z(r).start()
    att[z] = a_send[0]
    for r in (1, 3, 2):
        attended_z(r).wait_recv()
    mixed = lax.dot_general(
        att[...].reshape(HEADS * HEAD_DIM, ROWS),
        w_ref[...],
        (((0,), (0,)), ((), ())),
        preferred_element_type=jnp.float32,
    )
    out_ref[...] = mixed.astype(jnp.bfloat16)

    for r in (1, 2, 3):
        for copy in (queries_z, keys_z, queries_y, keys_x, stats_y, parts_y, attended_z):
            copy(r).wait_send()
    for r in range(4):
        keys_core(r).wait_send()


def on_device(queries, keys, values, valid, out_weight):
    flags = (valid > 0).astype(jnp.bfloat16)
    kept = (keys * flags[:, None]).reshape(ROWS, GROUPS, GH, HEAD_DIM)
    first = kept[:, :, :2].reshape(ROWS, GROUPS, ROWS).transpose(1, 0, 2)
    second = jnp.concatenate([kept[:, :, 2], kept[:, :, 2]], axis=-1).transpose(1, 0, 2)
    value_rows = (values * flags[:, None]).T.reshape(GROUPS, GD, ROWS)
    flag_rows = jnp.broadcast_to(
        jnp.concatenate([flags[None, :], jnp.zeros((15, ROWS), jnp.bfloat16)])[None],
        (GROUPS, 16, ROWS),
    )
    kv_src = jnp.concatenate([first, second, value_rows, flag_rows], axis=1)
    q_src = queries.T.reshape(GROUPS, GD, ROWS)
    bf16, f32 = jnp.bfloat16, jnp.float32
    whole = pl.BlockSpec(memory_space=pltpu.VMEM)
    return pl.pallas_call(
        kernel,
        out_shape=jax.ShapeDtypeStruct((ROWS, HEADS * HEAD_DIM), bf16),
        in_specs=[whole] * 3,
        out_specs=whole,
        scratch_shapes=[
            pltpu.VMEM((2, 4, 4, SHARD, ROWS), bf16),
            pltpu.VMEM((4, 4, GD, ROWS), bf16),
            pltpu.VMEM((2, 2 * ROWS, 4 * TILE), bf16),
            pltpu.VMEM((ROWS, 4 * TILE), bf16),
            pltpu.VMEM((GH, 8 * ROWS, TILE), f32),
            pltpu.VMEM((GH, HEAD_DIM + 16, 4 * TILE), f32),
            pltpu.VMEM((GH, 1, 4 * TILE), f32),
            pltpu.VMEM((GH, 1, TILE), f32),
            pltpu.VMEM((4, GD, TILE), bf16),
            pltpu.VMEM((4, 8, TILE), f32),
            pltpu.VMEM((4, GD, TILE), bf16),
            pltpu.VMEM((4, 8, TILE), f32),
            pltpu.VMEM((4, GD, ROWS), bf16),
            pltpu.VMEM((4, GD, ROWS), bf16),
            pltpu.SemaphoreType.DMA((32,)),
            pltpu.SemaphoreType.DMA((32,)),
        ],
        compiler_params=pltpu.CompilerParams(
            collective_id=0, has_side_effects=True, vmem_limit_bytes=56 << 20
        ),
        name="attend",
    )(kv_src, q_src, out_weight)


def solution(mesh):
    return jax.shard_map(
        on_device,
        mesh=mesh,
        in_specs=(
            P(("blk", "inner"), None),
            P(("blk", "inner"), None),
            P(("blk", "inner"), None),
            P(("blk", "inner")),
            P(),
        ),
        out_specs=P(("blk", "inner"), None),
        check_vma=False,
    )
```

```python
import jax
import jax.numpy as jnp
from jax import lax
from jax.experimental import pallas as pl
from jax.experimental.pallas import tpu as pltpu
from jax.sharding import PartitionSpec as P

HEADS = 12
HEAD_DIM = 64
GROUPS = 4
GH = HEADS // GROUPS
ROWS = 128
GD = GH * HEAD_DIM
TILE = 4 * ROWS
KROWS = ROWS + HEAD_DIM
SHARD = KROWS + GD + 16
PART = GD + 16
LOG2E = 1.4426950408889634
MESH = pl.DeviceIdType.MESH

KA, QA, QY, QZ, KX, KF, KC, KS, OP = 0, 4, 8, 12, 16, 24, 28, 32, 36
COPIES = OP + 16


def kernel(
    q_ref, k_ref, v_ref, valid_ref, out_ref,
    kv_src, q_src, kv, qb, qs, sb, acc, top, shrink, cur, stat, o_send, o_recv,
    send_sem, recv_sem,
):
    bf16, f32 = jnp.bfloat16, jnp.float32
    blk = lax.axis_index("blk")
    inner = lax.axis_index("inner")
    y, x, c = blk % 4, inner // 4, inner % 2
    z = (inner // 2 % 2) * 2 + blk // 4

    def at(dx=0, dy=0, dz=0, dc=0):
        tx, ty, tz, tc = (x + dx) % 4, (y + dy) % 4, (z + dz) % 4, (c + dc) % 2
        return ((tz % 2) * 4 + ty, tx * 4 + (tz // 2) * 2 + tc)

    def send(src, dst, number, device):
        return pltpu.make_async_remote_copy(
            src_ref=src, dst_ref=dst, send_sem=send_sem.at[number], recv_sem=recv_sem.at[number],
            device_id=device, device_id_type=MESH,
        )

    def keys_z(r):
        return send(kv_src.at[(z + r) % 4], kv.at[0, 0, r], KA + r, at(dz=r))

    def queries_z(r):
        return send(q_src.at[(z + r) % 4], qb.at[0, r], QA + r, at(dz=r))

    def queries_y_own(r):
        return send(qb.at[0, 0], qb.at[r, 0], QY + r, at(dy=r))

    def queries_y(r):
        return send(qb.at[0, pl.ds(1, 3)], qb.at[r, pl.ds(1, 3)], QZ + r, at(dy=r))

    def keys_up(rz):
        return send(kv.at[0, 0, rz], kv.at[0, 1, rz], KX + rz, at(dx=1))

    def keys_down(rz):
        return send(kv.at[0, 0, rz], kv.at[0, 3, rz], KX + 4 + rz, at(dx=3))

    def keys_on(rz):
        if rz < 2:
            return send(kv.at[0, 1, rz], kv.at[0, 2, rz], KF + rz, at(dx=1))
        return send(kv.at[0, 3, rz], kv.at[0, 2, rz], KF + rz, at(dx=3))

    def keys_core_own(rz):
        return send(kv.at[0, 0, rz], kv.at[1, 0, rz], KC + rz, at(dc=1))

    def keys_core(rx):
        return send(kv.at[0, rx], kv.at[1, rx], KS + rx, at(dc=1))

    def part(ry, rz):
        return send(
            o_send.at[ry, rz], o_recv.at[ry, rz], OP + 4 * ry + rz, at(dy=4 - ry, dz=4 - rz)
        )

    barrier = pltpu.get_barrier_semaphore()
    partners = [at(dc=1), at(dx=1), at(dx=3)]
    partners += [at(dy=ry, dz=rz) for ry in range(4) for rz in range(4) if ry or rz]
    for device in partners:
        pl.semaphore_signal(barrier, inc=1, device_id=device, device_id_type=MESH)

    turned = q_ref[...].T
    for g in range(GROUPS):
        q_src[g] = turned[g * GD : (g + 1) * GD]
    qb[0, 0] = q_src[z]

    pl.semaphore_wait(barrier, len(partners))
    for r in (1, 3, 2):
        queries_z(r).start()
    for r in (1, 3, 2):
        queries_y_own(r).start()

    flag_row = jnp.where(valid_ref[...] > 0, 1.0, 0.0).astype(f32)
    flag_square = jnp.broadcast_to(flag_row, (ROWS, ROWS))
    key_flags = flag_square.T.astype(bf16)
    value_flags = flag_square[:1].astype(bf16)
    first_row = lax.broadcasted_iota(jnp.int32, (16, ROWS), 0) == 0
    flag_rows = jnp.where(first_row, jnp.broadcast_to(flag_row, (16, ROWS)), 0.0).astype(bf16)
    turned = v_ref[...].T
    for g in range(GROUPS):
        kv_src[g, :ROWS, :] = k_ref[:, g * GD : g * GD + ROWS] * key_flags
        third = k_ref[:, g * GD + ROWS : (g + 1) * GD] * key_flags[:, :HEAD_DIM]
        kv_src[g, ROWS:KROWS, :] = jnp.concatenate([third[:HEAD_DIM], third[HEAD_DIM:]], axis=1)
        kv_src[g, KROWS : KROWS + GD, :] = turned[g * GD : (g + 1) * GD] * value_flags
        kv_src[g, KROWS + GD :, :] = flag_rows
    kv[0, 0, 0] = kv_src[z]
    for r in (1, 3, 2):
        keys_z(r).start()

    def spread(rz):
        keys_up(rz).start()
        keys_down(rz).start()
        keys_core_own(rz).start()

    spread(0)
    qs[...] = jnp.zeros_like(qs)
    acc[...] = jnp.zeros_like(acc)
    top[...] = jnp.zeros_like(top)

    def prepare(ry):
        for rz in range(4):
            columns = pl.ds(ry * TILE + rz * ROWS, ROWS)
            scaled = qb[ry, rz].astype(f32) * (LOG2E * HEAD_DIM**-0.5)
            high = scaled.astype(bf16)
            low = (scaled - high.astype(f32)).astype(bf16)
            for n, h, at_row in ((0, 0, 0), (1, 1, 1), (2, 2, 0), (3, 2, 1)):
                rows = slice(h * HEAD_DIM, (h + 1) * HEAD_DIM)
                qs[n, at_row * HEAD_DIM : (at_row + 1) * HEAD_DIM, columns] = high[rows]
                qs[n, ROWS + at_row * HEAD_DIM : ROWS + (at_row + 1) * HEAD_DIM, columns] = low[
                    rows
                ]

    for r in (1, 3, 2):
        queries_z(r).wait_recv()
    for r in (1, 3, 2):
        queries_y(r).start()
    prepare(0)
    for r in (1, 3, 2):
        keys_z(r).wait_recv()
        spread(r)
    for rz in (0, 1, 3, 2):
        keys_core_own(rz).wait_recv()

    def gray(p):
        return p + (p // 2) * (1 - 2 * (p % 2))

    def place(g):
        if isinstance(g, int) and g < 4:
            return 0, gray(g)
        late = g // 8
        p = (g - 4) * (1 - late) + ((g - 8) // 2) * late
        return 1 + late * (2 - g % 2), gray(p + late * (3 - 2 * p))

    def tile(ry):
        return pl.ds(pl.multiple_of(ry * TILE, TILE), TILE)

    def score(g, h):
        rx, ry = place(g)
        columns = tile(ry)
        rows = slice(0, ROWS) if h < 2 else slice(ROWS, KROWS)
        keys = jnp.concatenate(
            [kv[cc, rx, rz, rows, :] for cc in range(2) for rz in range(4)], axis=0
        )
        keys = jnp.concatenate([keys, keys], axis=1)
        if h < 2:
            s = jnp.dot(keys, qs[h, :, columns], preferred_element_type=f32)
            sb[h] = s.reshape(8, 2, HEAD_DIM, TILE)
            most = jnp.max(s, axis=0, keepdims=True)
        else:
            sa = jnp.dot(keys, qs[2, :, columns], preferred_element_type=f32)
            sb[h, :, 0] = sa.reshape(8, HEAD_DIM, TILE)
            sc = jnp.dot(keys, qs[3, :, columns], preferred_element_type=f32)
            sb[h, :, 1] = sc.reshape(8, HEAD_DIM, TILE)
            most = jnp.maximum(
                jnp.max(sa, axis=0, keepdims=True), jnp.max(sc, axis=0, keepdims=True)
            )
        old = top[h, :, columns]
        new = jnp.maximum(old, most)
        shrink[h] = jnp.exp2(old - new)
        top[h, :, columns] = new
        cur[h] = new

    def weigh(g, h):
        rx, ry = place(g)
        columns = tile(ry)
        chances = jnp.exp2(sb[h].reshape(8 * ROWS, TILE) - cur[h]).astype(bf16)
        first = KROWS + h * HEAD_DIM
        values = jnp.concatenate(
            [
                jnp.concatenate(
                    [kv[cc, rx, rz, first : first + HEAD_DIM, :], kv[cc, rx, rz, KROWS + GD :, :]],
                    axis=0,
                )
                for cc in range(2)
                for rz in range(4)
            ],
            axis=1,
        )
        acc[h, :, columns] = acc[h, :, columns] * shrink[h] + jnp.dot(
            values, chances, preferred_element_type=f32
        )

    def step(g, between=None):
        score(g, 1)
        weigh(g, 0)
        score(g, 2)
        weigh(g, 1)
        if between is not None:
            between()
        if not isinstance(g, int) or g < 15:
            score(g + 1, 0)
        weigh(g, 2)

    def deliver(ry):
        columns = pl.ds(ry * TILE, TILE)
        stat[...] = jnp.zeros_like(stat)
        for h in range(GH):
            left = top[h, :, columns]
            for n in range(3):
                piece = left.astype(bf16).astype(f32)
                stat[n * GH + h : n * GH + h + 1, :] = piece
                left = left - piece
            left = acc[h, HEAD_DIM : HEAD_DIM + 1, columns]
            for n in range(3, 5):
                piece = left.astype(bf16).astype(f32)
                stat[n * GH + h : n * GH + h + 1, :] = piece
                left = left - piece
        for rz in (2, 1, 3, 0):
            to = o_send if ry or rz else o_recv
            columns = pl.ds(ry * TILE + rz * ROWS, ROWS)
            for h in range(GH):
                to[ry, rz, h * HEAD_DIM : (h + 1) * HEAD_DIM, :] = acc[
                    h, :HEAD_DIM, columns
                ].astype(bf16)
            to[ry, rz, GD:, :] = stat[:, rz * ROWS : (rz + 1) * ROWS].astype(bf16)
            if ry or rz:
                part(ry, rz).start()

    def queries_in(ry):
        queries_y_own(ry).wait_recv()
        queries_y(ry).wait_recv()
        prepare(ry)

    score(0, 0)
    step(0, lambda: queries_in(1))
    for rz in (0, 1):
        keys_up(rz).wait_recv()
        keys_on(rz).start()
    keys_down(3).wait_recv()
    keys_on(3).start()
    step(1, lambda: queries_in(3))
    keys_down(2).wait_recv()
    keys_on(2).start()
    for rz in (2, 3):
        keys_up(rz).wait_recv()
    keys_core(1).start()
    for rz in (0, 1):
        keys_down(rz).wait_recv()
    keys_core(3).start()
    step(2, lambda: queries_in(2))
    step(3, lambda: keys_core(1).wait_recv())

    def loop(g, carry):
        @pl.when(g == 5)
        def _():
            for rz in range(4):
                keys_on(rz).wait_recv()
            keys_core(2).start()

        @pl.when(g == 7)
        def _():
            keys_core(3).wait_recv()

        @pl.when(g == 8)
        def _():
            keys_core(2).wait_recv()

        step(g)

        for n, ry in ((9, 2), (11, 3), (13, 1)):

            @pl.when(g == n)
            def _():
                deliver(ry)

        return carry

    lax.fori_loop(4, 15, loop, 0)
    step(15)
    deliver(0)

    for rz in (0, 1, 3, 2):
        for ry in (2, 3, 1, 0):
            if ry or rz:
                part(ry, rz).wait_recv()
        stats = [o_recv[ry, rz, GD:, :].astype(f32) for ry in range(4)]
        for h in range(GH):
            rows = slice(h * HEAD_DIM, (h + 1) * HEAD_DIM)
            row = [[st[n * GH + h : n * GH + h + 1] for n in range(5)] for st in stats]
            tops = [r[0] + r[1] + r[2] for r in row]
            most = jnp.maximum(jnp.maximum(tops[0], tops[1]), jnp.maximum(tops[2], tops[3]))
            total = jnp.exp2(-most)
            weighted = jnp.zeros((HEAD_DIM, ROWS), f32)
            for ry in range(4):
                factor = jnp.exp2(tops[ry] - most)
                total = total + (row[ry][3] + row[ry][4]) * factor
                weighted = weighted + o_recv[ry, rz, rows, :].astype(f32) * factor
            out_ref[(z + rz) % 4, rows, :] = (weighted / total).astype(bf16)

    for r in (1, 2, 3):
        for copy in (queries_z, keys_z, queries_y_own, queries_y, keys_core):
            copy(r).wait_send()
    for r in range(4):
        for copy in (keys_up, keys_down, keys_on, keys_core_own):
            copy(r).wait_send()
        for ry in range(4):
            if ry or r:
                part(ry, r).wait_send()


def on_device(queries, keys, values, valid, out_weight):
    bf16, f32 = jnp.bfloat16, jnp.float32
    whole = pl.BlockSpec(memory_space=pltpu.VMEM)
    attended = pl.pallas_call(
        kernel,
        out_shape=jax.ShapeDtypeStruct((GROUPS, GD, ROWS), bf16),
        in_specs=[whole] * 4,
        out_specs=whole,
        scratch_shapes=[
            pltpu.VMEM((GROUPS, SHARD, ROWS), bf16),
            pltpu.VMEM((GROUPS, GD, ROWS), bf16),
            pltpu.VMEM((2, 4, 4, SHARD, ROWS), bf16),
            pltpu.VMEM((4, 4, GD, ROWS), bf16),
            pltpu.VMEM((4, 2 * ROWS, 4 * TILE), bf16),
            pltpu.VMEM((GH, 8, 2, HEAD_DIM, TILE), f32),
            pltpu.VMEM((GH, HEAD_DIM + 16, 4 * TILE), f32),
            pltpu.VMEM((GH, 1, 4 * TILE), f32),
            pltpu.VMEM((GH, 1, TILE), f32),
            pltpu.VMEM((GH, 1, TILE), f32),
            pltpu.VMEM((16, TILE), f32),
            pltpu.VMEM((4, 4, PART, ROWS), bf16),
            pltpu.VMEM((4, 4, PART, ROWS), bf16),
            pltpu.SemaphoreType.DMA((COPIES,)),
            pltpu.SemaphoreType.DMA((COPIES,)),
        ],
        compiler_params=pltpu.CompilerParams(
            collective_id=0, has_side_effects=True, vmem_limit_bytes=56 << 20
        ),
        name="attend",
    )(queries, keys, values, valid.reshape(1, ROWS))
    mixed = lax.dot_general(
        attended.reshape(HEADS * HEAD_DIM, ROWS),
        out_weight,
        (((0,), (0,)), ((), ())),
        preferred_element_type=f32,
    )
    return mixed.astype(bf16)


def solution(mesh):
    return jax.shard_map(
        on_device,
        mesh=mesh,
        in_specs=(
            P(("blk", "inner"), None),
            P(("blk", "inner"), None),
            P(("blk", "inner"), None),
            P(("blk", "inner")),
            P(),
        ),
        out_specs=P(("blk", "inner"), None),
        check_vma=False,
    )
```

```python
import jax
import jax.numpy as jnp
from jax import lax
from jax.experimental import pallas as pl
from jax.experimental.pallas import tpu as pltpu
from jax.sharding import PartitionSpec as P

HEADS = 12
HEAD_DIM = 64
GROUPS = 4
GH = HEADS // GROUPS
ROWS = 128
GD = GH * HEAD_DIM
TILE = 4 * ROWS
KROWS = ROWS + HEAD_DIM
SHARD = KROWS + GD + 16
PART = HEAD_DIM + 16
LOG2E = 1.4426950408889634
MESH = pl.DeviceIdType.MESH

KA, QA, QY, QZ, KX, KF, KC, KS, OP, OH = 0, 4, 8, 12, 16, 24, 28, 32, 36, 52
COPIES = OH + 12

KEY_SLOT = {(rx, rz): 4 * rx + rz for rx in range(4) for rz in range(4)}
KEY_SLOT.update({(0, 2): 4, (1, 0): 2, (3, 0): 6, (1, 2): 12})
QUERY_SLOT = {(ry, rz): 4 * ry + rz for ry in range(4) for rz in range(4)}
QUERY_SLOT.update({(0, 2): 4, (1, 0): 2})
TILES = [[owner for owner, n in QUERY_SLOT.items() if n // 4 == t] for t in range(4)]
CHUNK_AT = (0, 0, 0, 0, 1, 1, 1, 1, 3, 3, 2, 2, 3, 2, 3, 2)
TILE_AT = (0, 1, 3, 2, 0, 1, 3, 2, 2, 3, 2, 3, 1, 1, 0, 0)


def lookup(table, g):
    if isinstance(g, int):
        return table[g]
    packed = sum(n << 2 * i for i, n in enumerate(table[4:]))
    return lax.shift_right_logical(jnp.int32(packed), 2 * (g - 4)) % 4


def kernel(
    q_ref, k_ref, v_ref, valid_ref, out_ref,
    kv_src, q_src, kv, qb, qs, sb, acc, top, shrink, cur, stat, o_send, o_recv,
    send_sem, recv_sem,
):
    bf16, f32 = jnp.bfloat16, jnp.float32
    blk = lax.axis_index("blk")
    inner = lax.axis_index("inner")
    y, x, c = blk % 4, inner // 4, inner % 2
    z = (inner // 2 % 2) * 2 + blk // 4

    def at(dx=0, dy=0, dz=0, dc=0):
        tx, ty, tz, tc = (x + dx) % 4, (y + dy) % 4, (z + dz) % 4, (c + dc) % 2
        return ((tz % 2) * 4 + ty, tx * 4 + (tz // 2) * 2 + tc)

    def send(src, dst, number, device):
        return pltpu.make_async_remote_copy(
            src_ref=src, dst_ref=dst, send_sem=send_sem.at[number], recv_sem=recv_sem.at[number],
            device_id=device, device_id_type=MESH,
        )

    def keys(cc, rx, rz):
        return kv.at[cc, KEY_SLOT[rx, rz]]

    def keys_z(r):
        return send(kv_src.at[(z + r) % 4], keys(0, 0, r), KA + r, at(dz=r))

    def queries_z(r):
        return send(q_src.at[(z + r) % 4], qb.at[0, r], QA + r, at(dz=r))

    def queries_y_own(r):
        return send(qb.at[0, 0], qb.at[r, 0], QY + r, at(dy=r))

    def queries_y(r):
        return send(qb.at[0, pl.ds(1, 3)], qb.at[r, pl.ds(1, 3)], QZ + r, at(dy=r))

    def keys_up(rz):
        return send(keys(0, 0, rz), keys(0, 1, rz), KX + rz, at(dx=1))

    def keys_down(rz):
        return send(keys(0, 0, rz), keys(0, 3, rz), KX + 4 + rz, at(dx=3))

    def keys_on(rz):
        if rz < 2:
            return send(keys(0, 1, rz), keys(0, 2, rz), KF + rz, at(dx=1))
        return send(keys(0, 3, rz), keys(0, 2, rz), KF + rz, at(dx=3))

    def keys_core_first(n):
        return send(kv.at[0, n], kv.at[1, n], KC + n, at(dc=1))

    def keys_core(t):
        slots = pl.ds(4 * t, 4)
        return send(kv.at[0, slots], kv.at[1, slots], KS + t, at(dc=1))

    def part(ry, rz):
        device = at(dy=4 - ry, dz=4 - rz)
        return send(o_send.at[ry, rz], o_recv.at[ry, rz], OP + 4 * ry + rz, device)

    def part_head(ry, rz, h):
        device = at(dy=4 - ry, dz=4 - rz)
        number = OH + 4 * h + QUERY_SLOT[ry, rz]
        return send(o_send.at[ry, rz, h], o_recv.at[ry, rz, h], number, device)

    barrier = pltpu.get_barrier_semaphore()
    partners = [at(dc=1), at(dx=1), at(dx=3)]
    partners += [at(dy=ry, dz=rz) for ry in range(4) for rz in range(4) if ry or rz]
    for device in partners:
        pl.semaphore_signal(barrier, inc=1, device_id=device, device_id_type=MESH)

    turned = q_ref[...].T
    for g in range(GROUPS):
        q_src[g] = turned[g * GD : (g + 1) * GD]
    qb[0, 0] = q_src[z]

    pl.semaphore_wait(barrier, len(partners))
    for r in (1, 3, 2):
        queries_z(r).start()
    for r in (1, 3, 2):
        queries_y_own(r).start()

    flag_row = jnp.where(valid_ref[...] > 0, 1.0, 0.0).astype(f32)
    flag_square = jnp.broadcast_to(flag_row, (ROWS, ROWS))
    key_flags = flag_square.T.astype(bf16)
    value_flags = flag_square[:1].astype(bf16)
    first_row = lax.broadcasted_iota(jnp.int32, (16, ROWS), 0) == 0
    flag_rows = jnp.where(first_row, jnp.broadcast_to(flag_row, (16, ROWS)), 0.0).astype(bf16)
    turned = v_ref[...].T
    for g in range(GROUPS):
        kv_src[g, :ROWS, :] = k_ref[:, g * GD : g * GD + ROWS] * key_flags
        third = k_ref[:, g * GD + ROWS : (g + 1) * GD] * key_flags[:, :HEAD_DIM]
        kv_src[g, ROWS:KROWS, :] = jnp.concatenate([third[:HEAD_DIM], third[HEAD_DIM:]], axis=1)
        kv_src[g, KROWS : KROWS + GD, :] = turned[g * GD : (g + 1) * GD] * value_flags
        kv_src[g, KROWS + GD :, :] = flag_rows
    kv[0, KEY_SLOT[0, 0]] = kv_src[z]
    for r in (1, 3):
        keys_z(r).start()
    keys_up(0).start()
    keys_down(0).start()
    keys_core_first(0).start()
    qs[...] = jnp.zeros_like(qs)
    acc[...] = jnp.zeros_like(acc)
    top[...] = jnp.zeros_like(top)
    stat[...] = jnp.zeros_like(stat)

    def prepare(t):
        for ry, rz in TILES[t]:
            columns = pl.ds(QUERY_SLOT[ry, rz] * ROWS, ROWS)
            scaled = qb[ry, rz].astype(f32) * (LOG2E * HEAD_DIM**-0.5)
            high = scaled.astype(bf16)
            low = (scaled - high.astype(f32)).astype(bf16)
            for n, h, at_row in ((0, 0, 0), (1, 1, 1), (2, 2, 0), (3, 2, 1)):
                rows = slice(h * HEAD_DIM, (h + 1) * HEAD_DIM)
                qs[n, at_row * HEAD_DIM : (at_row + 1) * HEAD_DIM, columns] = high[rows]
                qs[n, ROWS + at_row * HEAD_DIM : ROWS + (at_row + 1) * HEAD_DIM, columns] = low[
                    rows
                ]

    for r in (1, 3, 2):
        queries_z(r).wait_recv()
    for r in (1, 3, 2):
        queries_y(r).start()
    queries_y_own(1).wait_recv()
    prepare(0)
    for r in (1, 3):
        keys_z(r).wait_recv()
        keys_core_first(KEY_SLOT[0, r]).start()
        keys_up(r).start()
        keys_down(r).start()
    keys_z(2).start()
    keys_up(0).wait_recv()
    keys_core_first(KEY_SLOT[1, 0]).start()
    keys_on(0).start()
    for n in (0, 1, 3, 2):
        keys_core_first(n).wait_recv()

    def tile(ry):
        return pl.ds(pl.multiple_of(ry * TILE, TILE), TILE)

    def score(g, h):
        chunk = 4 * lookup(CHUNK_AT, g)
        columns = tile(lookup(TILE_AT, g))
        rows = slice(0, ROWS) if h < 2 else slice(ROWS, KROWS)
        keys = jnp.concatenate(
            [kv[cc, chunk + n, rows, :] for cc in range(2) for n in range(4)], axis=0
        )
        keys = jnp.concatenate([keys, keys], axis=1)
        if h < 2:
            s = jnp.dot(keys, qs[h, :, columns], preferred_element_type=f32)
            sb[h] = s.reshape(8, 2, HEAD_DIM, TILE)
            most = jnp.max(s, axis=0, keepdims=True)
        else:
            sa = jnp.dot(keys, qs[2, :, columns], preferred_element_type=f32)
            sb[h, :, 0] = sa.reshape(8, HEAD_DIM, TILE)
            sc = jnp.dot(keys, qs[3, :, columns], preferred_element_type=f32)
            sb[h, :, 1] = sc.reshape(8, HEAD_DIM, TILE)
            most = jnp.maximum(
                jnp.max(sa, axis=0, keepdims=True), jnp.max(sc, axis=0, keepdims=True)
            )
        old = top[h, :, columns]
        new = jnp.maximum(old, most)
        shrink[h] = jnp.exp2(old - new)
        top[h, :, columns] = new
        cur[h] = new

    def weigh(g, h):
        chunk = 4 * lookup(CHUNK_AT, g)
        columns = tile(lookup(TILE_AT, g))
        chances = jnp.exp2(sb[h].reshape(8 * ROWS, TILE) - cur[h]).astype(bf16)
        first = KROWS + h * HEAD_DIM
        values = jnp.concatenate(
            [
                jnp.concatenate(
                    [
                        kv[cc, chunk + n, first : first + HEAD_DIM, :],
                        kv[cc, chunk + n, KROWS + GD :, :],
                    ],
                    axis=0,
                )
                for cc in range(2)
                for n in range(4)
            ],
            axis=1,
        )
        acc[h, :, columns] = acc[h, :, columns] * shrink[h] + jnp.dot(
            values, chances, preferred_element_type=f32
        )

    def step(g, between=None):
        score(g, 1)
        weigh(g, 0)
        score(g, 2)
        weigh(g, 1)
        if between is not None:
            between()
        score(g + 1, 0)
        weigh(g, 2)

    def pack(t, h):
        columns = pl.ds(t * TILE, TILE)
        left = top[h, :, columns]
        for n in range(3):
            piece = left.astype(bf16).astype(f32)
            stat[h, n : n + 1, :] = piece
            left = left - piece
        left = acc[h, HEAD_DIM : HEAD_DIM + 1, columns]
        for n in range(3, 5):
            piece = left.astype(bf16).astype(f32)
            stat[h, n : n + 1, :] = piece
            left = left - piece
        for ry, rz in TILES[t]:
            to = o_send if ry or rz else o_recv
            first = QUERY_SLOT[ry, rz] * ROWS
            to[ry, rz, h, :HEAD_DIM, :] = acc[h, :HEAD_DIM, pl.ds(first, ROWS)].astype(bf16)
            first = first - t * TILE
            to[ry, rz, h, HEAD_DIM:, :] = stat[h, :, first : first + ROWS].astype(bf16)

    def deliver(t):
        for h in range(GH):
            pack(t, h)
        for ry, rz in TILES[t]:
            part(ry, rz).start()

    def deliver_last(h):
        pack(0, h)
        for ry, rz in TILES[0][1:]:
            part_head(ry, rz, h).start()

    def queries_in(ry):
        if ry > 1:
            queries_y_own(ry).wait_recv()
        queries_y(ry).wait_recv()
        prepare(ry)

    score(0, 0)
    step(0, lambda: queries_in(1))
    keys_up(1).wait_recv()
    keys_on(1).start()
    step(1, lambda: queries_in(3))
    keys_z(2).wait_recv()
    keys_up(2).start()
    keys_down(2).start()
    keys_down(3).wait_recv()
    keys_on(3).start()
    keys_up(3).wait_recv()
    keys_down(0).wait_recv()
    keys_core(1).start()
    step(2, lambda: queries_in(2))
    step(3, lambda: keys_core(1).wait_recv())

    def loop(g, carry):
        @pl.when(g == 5)
        def _():
            keys_down(2).wait_recv()
            keys_on(2).start()
            keys_up(2).wait_recv()
            keys_down(1).wait_recv()
            keys_core(3).start()

        @pl.when(g == 7)
        def _():
            keys_core(3).wait_recv()

        @pl.when(g == 8)
        def _():
            for rz in range(4):
                keys_on(rz).wait_recv()
            keys_core(2).start()

        @pl.when(g == 9)
        def _():
            keys_core(2).wait_recv()

        step(g)

        for n, t in ((10, 2), (11, 3), (13, 1)):

            @pl.when(g == n)
            def _():
                deliver(t)

        return carry

    lax.fori_loop(4, 15, loop, 0)
    score(15, 1)
    weigh(15, 0)
    score(15, 2)
    deliver_last(0)
    weigh(15, 1)
    deliver_last(1)
    weigh(15, 2)
    deliver_last(2)

    for t in (2, 3, 1):
        for ry, rz in TILES[t]:
            part(ry, rz).wait_recv()
    for h in range(GH):
        for ry, rz in TILES[0][1:]:
            part_head(ry, rz, h).wait_recv()
        for rz in range(4):
            stats = [o_recv[ry, rz, h, HEAD_DIM:, :].astype(f32) for ry in range(4)]
            row = [[st[n : n + 1] for n in range(5)] for st in stats]
            tops = [r[0] + r[1] + r[2] for r in row]
            most = jnp.maximum(jnp.maximum(tops[0], tops[1]), jnp.maximum(tops[2], tops[3]))
            total = jnp.exp2(-most)
            weighted = jnp.zeros((HEAD_DIM, ROWS), f32)
            for ry in range(4):
                factor = jnp.exp2(tops[ry] - most)
                total = total + (row[ry][3] + row[ry][4]) * factor
                weighted = weighted + o_recv[ry, rz, h, :HEAD_DIM, :].astype(f32) * factor
            rows = slice(h * HEAD_DIM, (h + 1) * HEAD_DIM)
            out_ref[(z + rz) % 4, rows, :] = (weighted / total).astype(bf16)

    for r in (1, 2, 3):
        for copy in (queries_z, keys_z, queries_y_own, queries_y, keys_core):
            copy(r).wait_send()
    for r in range(4):
        for copy in (keys_up, keys_down, keys_on, keys_core_first):
            copy(r).wait_send()
    for t in (1, 2, 3):
        for ry, rz in TILES[t]:
            part(ry, rz).wait_send()
    for h in range(GH):
        for ry, rz in TILES[0][1:]:
            part_head(ry, rz, h).wait_send()


def on_device(queries, keys, values, valid, out_weight):
    bf16, f32 = jnp.bfloat16, jnp.float32
    whole = pl.BlockSpec(memory_space=pltpu.VMEM)
    attended = pl.pallas_call(
        kernel,
        out_shape=jax.ShapeDtypeStruct((GROUPS, GD, ROWS), bf16),
        in_specs=[whole] * 4,
        out_specs=whole,
        scratch_shapes=[
            pltpu.VMEM((GROUPS, SHARD, ROWS), bf16),
            pltpu.VMEM((GROUPS, GD, ROWS), bf16),
            pltpu.VMEM((2, 16, SHARD, ROWS), bf16),
            pltpu.VMEM((4, 4, GD, ROWS), bf16),
            pltpu.VMEM((4, 2 * ROWS, 4 * TILE), bf16),
            pltpu.VMEM((GH, 8, 2, HEAD_DIM, TILE), f32),
            pltpu.VMEM((GH, HEAD_DIM + 16, 4 * TILE), f32),
            pltpu.VMEM((GH, 1, 4 * TILE), f32),
            pltpu.VMEM((GH, 1, TILE), f32),
            pltpu.VMEM((GH, 1, TILE), f32),
            pltpu.VMEM((GH, 16, TILE), f32),
            pltpu.VMEM((4, 4, GH, PART, ROWS), bf16),
            pltpu.VMEM((4, 4, GH, PART, ROWS), bf16),
            pltpu.SemaphoreType.DMA((COPIES,)),
            pltpu.SemaphoreType.DMA((COPIES,)),
        ],
        compiler_params=pltpu.CompilerParams(
            collective_id=0, has_side_effects=True, vmem_limit_bytes=56 << 20
        ),
        name="attend",
    )(queries, keys, values, valid.reshape(1, ROWS))
    mixed = lax.dot_general(
        attended.reshape(HEADS * HEAD_DIM, ROWS),
        out_weight,
        (((0,), (0,)), ((), ())),
        preferred_element_type=f32,
    )
    return mixed.astype(bf16)


def solution(mesh):
    return jax.shard_map(
        on_device,
        mesh=mesh,
        in_specs=(
            P(("blk", "inner"), None),
            P(("blk", "inner"), None),
            P(("blk", "inner"), None),
            P(("blk", "inner")),
            P(),
        ),
        out_specs=P(("blk", "inner"), None),
        check_vma=False,
    )
```

```python
import jax
import jax.numpy as jnp
from jax import lax
from jax.experimental import pallas as pl
from jax.experimental.pallas import tpu as pltpu
from jax.sharding import PartitionSpec as P

HEADS = 12
HEAD_DIM = 64
GROUPS = 4
GH = HEADS // GROUPS
ROWS = 128
GD = GH * HEAD_DIM
TILE = 4 * ROWS
KROWS = ROWS + HEAD_DIM
SHARD = KROWS + GD + 16
PART = GD + 16
LAST = HEAD_DIM + 16
LOG2E = 1.4426950408889634
MESH = pl.DeviceIdType.MESH

KA, QA, QY, KX, KF, KC, OP, OH = 0, 4, 8, 24, 32, 36, 52, 68
COPIES = OH + 12

CHUNKS = (
    ((0, 0), (0, 1), (1, 0), (0, 3)),
    ((3, 0), (1, 1), (3, 1), (0, 2)),
    ((1, 3), (3, 3), (1, 2), (3, 2)),
    ((2, 0), (2, 1), (2, 3), (2, 2)),
)
KEY_SLOT = {owner: 4 * t + n for t, chunk in enumerate(CHUNKS) for n, owner in enumerate(chunk)}
TILES = (
    ((0, 0), (0, 1), (0, 3), (1, 0)),
    ((0, 2), (1, 1), (3, 0), (2, 0)),
    ((2, 1), (2, 3), (2, 2), (3, 2)),
    ((3, 1), (1, 3), (3, 3), (1, 2)),
)
QUERY_SLOT = {owner: 4 * t + n for t, tile in enumerate(TILES) for n, owner in enumerate(tile)}
CHUNK_AT = (0, 0, 0, 0, 1, 1, 1, 2, 2, 2, 3, 3, 3, 1, 2, 3)
TILE_AT = (0, 1, 3, 2, 2, 3, 1, 2, 3, 1, 2, 3, 1, 0, 0, 0)


def lookup(table, g):
    if isinstance(g, int):
        return table[g]
    packed = sum(n << 2 * i for i, n in enumerate(table[4:]))
    return lax.shift_right_logical(jnp.int32(packed), 2 * (g - 4)) % 4


def kernel(
    q_ref, k_ref, v_ref, valid_ref, out_ref,
    kv_src, q_src, kv, qb, qs, sb, acc, top, shrink, cur, stat, stat_last, o_send, o_recv, h_send, h_recv,
    send_sem, recv_sem,
):
    bf16, f32 = jnp.bfloat16, jnp.float32
    blk = lax.axis_index("blk")
    inner = lax.axis_index("inner")
    y, x, c = blk % 4, inner // 4, inner % 2
    z = (inner // 2 % 2) * 2 + blk // 4

    def at(dx=0, dy=0, dz=0, dc=0):
        tx, ty, tz, tc = (x + dx) % 4, (y + dy) % 4, (z + dz) % 4, (c + dc) % 2
        return ((tz % 2) * 4 + ty, tx * 4 + (tz // 2) * 2 + tc)

    def send(src, dst, number, device):
        return pltpu.make_async_remote_copy(
            src_ref=src, dst_ref=dst, send_sem=send_sem.at[number], recv_sem=recv_sem.at[number],
            device_id=device, device_id_type=MESH,
        )

    def keys(cc, rx, rz):
        return kv.at[cc, KEY_SLOT[rx, rz]]

    def keys_z(r):
        return send(kv_src.at[(z + r) % 4], keys(0, 0, r), KA + r, at(dz=r))

    def queries_z(r):
        return send(q_src.at[(z + r) % 4], qb.at[0, r], QA + r, at(dz=r))

    def queries_y(ry, rz):
        return send(qb.at[0, rz], qb.at[ry, rz], QY + 4 * ry + rz, at(dy=ry))

    def keys_up(rz):
        return send(keys(0, 0, rz), keys(0, 1, rz), KX + rz, at(dx=1))

    def keys_down(rz):
        return send(keys(0, 0, rz), keys(0, 3, rz), KX + 4 + rz, at(dx=3))

    def keys_on(rz):
        if rz in (0, 3):
            return send(keys(0, 1, rz), keys(0, 2, rz), KF + rz, at(dx=1))
        return send(keys(0, 3, rz), keys(0, 2, rz), KF + rz, at(dx=3))

    def keys_core(rx, rz):
        return send(keys(0, rx, rz), keys(1, rx, rz), KC + KEY_SLOT[rx, rz], at(dc=1))

    def part(ry, rz):
        n = QUERY_SLOT[ry, rz]
        return send(o_send.at[n], o_recv.at[n], OP + n, at(dy=4 - ry, dz=4 - rz))

    def part_head(ry, rz, h):
        n = QUERY_SLOT[ry, rz]
        return send(h_send.at[n, h], h_recv.at[n, h], OH + 4 * h + n, at(dy=4 - ry, dz=4 - rz))

    barrier = pltpu.get_barrier_semaphore()
    partners = [at(dc=1), at(dx=1), at(dx=3)]
    partners += [at(dy=ry, dz=rz) for ry in range(4) for rz in range(4) if ry or rz]
    for device in partners:
        pl.semaphore_signal(barrier, inc=1, device_id=device, device_id_type=MESH)

    turned = q_ref[...].T
    for g in range(GROUPS):
        q_src[g] = turned[g * GD : (g + 1) * GD]
    qb[0, 0] = q_src[z]

    pl.semaphore_wait(barrier, len(partners))
    for r in (1, 3, 2):
        queries_z(r).start()
    for r in (1, 3, 2):
        queries_y(r, 0).start()

    flag_row = jnp.where(valid_ref[...] > 0, 1.0, 0.0).astype(f32)
    flag_square = jnp.broadcast_to(flag_row, (ROWS, ROWS))
    key_flags = flag_square.T.astype(bf16)
    value_flags = flag_square[:1].astype(bf16)
    first_row = lax.broadcasted_iota(jnp.int32, (16, ROWS), 0) == 0
    flag_rows = jnp.where(first_row, jnp.broadcast_to(flag_row, (16, ROWS)), 0.0).astype(bf16)
    turned = v_ref[...].T
    for g in range(GROUPS):
        kv_src[g, :ROWS, :] = k_ref[:, g * GD : g * GD + ROWS] * key_flags
        third = k_ref[:, g * GD + ROWS : (g + 1) * GD] * key_flags[:, :HEAD_DIM]
        kv_src[g, ROWS:KROWS, :] = jnp.concatenate([third[:HEAD_DIM], third[HEAD_DIM:]], axis=1)
        kv_src[g, KROWS : KROWS + GD, :] = turned[g * GD : (g + 1) * GD] * value_flags
        kv_src[g, KROWS + GD :, :] = flag_rows
    kv[0, KEY_SLOT[0, 0]] = kv_src[z]
    for r in (1, 3):
        keys_z(r).start()
    keys_up(0).start()
    keys_down(0).start()
    keys_core(0, 0).start()
    qs[...] = jnp.zeros_like(qs)
    acc[...] = jnp.zeros_like(acc)
    top[...] = jnp.zeros_like(top)
    stat[...] = jnp.zeros_like(stat)
    stat_last[...] = jnp.zeros_like(stat_last)

    def prepare(t):
        for ry, rz in TILES[t]:
            columns = pl.ds(QUERY_SLOT[ry, rz] * ROWS, ROWS)
            scaled = qb[ry, rz].astype(f32) * (LOG2E * HEAD_DIM**-0.5)
            high = scaled.astype(bf16)
            low = (scaled - high.astype(f32)).astype(bf16)
            for n, h, at_row in ((0, 0, 0), (1, 1, 1), (2, 2, 0), (3, 2, 1)):
                rows = slice(h * HEAD_DIM, (h + 1) * HEAD_DIM)
                qs[n, at_row * HEAD_DIM : (at_row + 1) * HEAD_DIM, columns] = high[rows]
                qs[n, ROWS + at_row * HEAD_DIM : ROWS + (at_row + 1) * HEAD_DIM, columns] = low[
                    rows
                ]

    for r in (1, 3, 2):
        queries_z(r).wait_recv()
        queries_y(1, r).start()
        queries_y(3, r).start()
    queries_y(1, 0).wait_recv()
    prepare(0)
    for r in (1, 3, 2):
        queries_y(2, r).start()

    def keys_in(copy, rx, rz):
        copy(rz).wait_recv()
        keys_core(rx, rz).start()

    def chunk_in(t):
        for rx, rz in CHUNKS[t]:
            keys_core(rx, rz).wait_recv()

    for r in (1, 3):
        keys_in(keys_z, 0, r)
        keys_up(r).start()
        keys_down(r).start()
    keys_z(2).start()
    keys_in(keys_up, 1, 0)
    keys_on(0).start()
    keys_in(keys_down, 3, 0)
    chunk_in(0)

    def tile(ry):
        return pl.ds(pl.multiple_of(ry * TILE, TILE), TILE)

    def score(g, h):
        chunk = 4 * lookup(CHUNK_AT, g)
        columns = tile(lookup(TILE_AT, g))
        rows = slice(0, ROWS) if h < 2 else slice(ROWS, KROWS)
        keys = jnp.concatenate(
            [kv[cc, chunk + n, rows, :] for cc in range(2) for n in range(4)], axis=0
        )
        keys = jnp.concatenate([keys, keys], axis=1)
        if h < 2:
            s = jnp.dot(keys, qs[h, :, columns], preferred_element_type=f32)
            sb[h] = s.reshape(8, 2, HEAD_DIM, TILE)
            most = jnp.max(s, axis=0, keepdims=True)
        else:
            sa = jnp.dot(keys, qs[2, :, columns], preferred_element_type=f32)
            sb[h, :, 0] = sa.reshape(8, HEAD_DIM, TILE)
            sc = jnp.dot(keys, qs[3, :, columns], preferred_element_type=f32)
            sb[h, :, 1] = sc.reshape(8, HEAD_DIM, TILE)
            most = jnp.maximum(
                jnp.max(sa, axis=0, keepdims=True), jnp.max(sc, axis=0, keepdims=True)
            )
        old = top[h, :, columns]
        new = jnp.maximum(old, most)
        shrink[h] = jnp.exp2(old - new)
        top[h, :, columns] = new
        cur[h] = new

    def weigh(g, h):
        chunk = 4 * lookup(CHUNK_AT, g)
        columns = tile(lookup(TILE_AT, g))
        chances = jnp.exp2(sb[h].reshape(8 * ROWS, TILE) - cur[h]).astype(bf16)
        first = KROWS + h * HEAD_DIM
        values = jnp.concatenate(
            [
                jnp.concatenate(
                    [
                        kv[cc, chunk + n, first : first + HEAD_DIM, :],
                        kv[cc, chunk + n, KROWS + GD :, :],
                    ],
                    axis=0,
                )
                for cc in range(2)
                for n in range(4)
            ],
            axis=1,
        )
        acc[h, :, columns] = acc[h, :, columns] * shrink[h] + jnp.dot(
            values, chances, preferred_element_type=f32
        )

    def step(g, between=None):
        score(g, 1)
        weigh(g, 0)
        score(g, 2)
        weigh(g, 1)
        if between is not None:
            between()
        score(g + 1, 0)
        weigh(g, 2)

    def pieces(store, at_row, value, n):
        for i in range(n):
            piece = value.astype(bf16).astype(f32)
            store[at_row(i), :] = piece
            value = value - piece

    def deliver(t):
        columns = pl.ds(t * TILE, TILE)
        for h in range(GH):
            pieces(stat, lambda i: pl.ds(GH * i + h, 1), top[h, :, columns], 3)
            total = acc[h, HEAD_DIM : HEAD_DIM + 1, columns]
            pieces(stat, lambda i: pl.ds(GH * (i + 3) + h, 1), total, 2)
        for n, (ry, rz) in enumerate(TILES[t]):
            slot = 4 * t + n
            for h in range(GH):
                rows = pl.ds(h * HEAD_DIM, HEAD_DIM)
                o_send[slot, rows, :] = acc[h, :HEAD_DIM, pl.ds(slot * ROWS, ROWS)].astype(bf16)
            o_send[slot, GD:, :] = stat[:, n * ROWS : (n + 1) * ROWS].astype(bf16)
            part(ry, rz).start()

    def deliver_last(h):
        columns = pl.ds(0, TILE)
        store = stat_last.at[h]
        pieces(store, lambda i: pl.ds(i, 1), top[h, :, columns], 3)
        pieces(store, lambda i: pl.ds(i + 3, 1), acc[h, HEAD_DIM : HEAD_DIM + 1, columns], 2)
        for n in (1, 2, 3, 0):
            to = h_send if n else h_recv
            to[n, h, :HEAD_DIM, :] = acc[h, :HEAD_DIM, pl.ds(n * ROWS, ROWS)].astype(bf16)
            to[n, h, HEAD_DIM:, :] = stat_last[h, :, n * ROWS : (n + 1) * ROWS].astype(bf16)
            if n:
                part_head(*TILES[0][n], h).start()

    def queries_in(t):
        for ry, rz in TILES[t]:
            if ry:
                queries_y(ry, rz).wait_recv()
        prepare(t)

    score(0, 0)
    step(0, lambda: queries_in(1))
    keys_in(keys_z, 0, 2)
    keys_up(2).start()
    keys_down(2).start()
    step(1, lambda: queries_in(3))
    keys_in(keys_down, 3, 1)
    keys_on(1).start()
    keys_in(keys_up, 1, 1)
    step(2, lambda: queries_in(2))
    keys_in(keys_up, 1, 3)
    keys_on(3).start()
    keys_in(keys_down, 3, 3)
    step(3, lambda: chunk_in(1))

    def loop(g, carry):
        @pl.when(g == 4)
        def _():
            keys_in(keys_down, 3, 2)
            keys_on(2).start()
            keys_in(keys_up, 1, 2)

        @pl.when(g == 5)
        def _():
            keys_in(keys_on, 2, 0)
            keys_in(keys_on, 2, 1)

        @pl.when(g == 8)
        def _():
            keys_in(keys_on, 2, 3)
            keys_in(keys_on, 2, 2)

        def between():
            for n, t in ((6, 2), (9, 3)):

                @pl.when(g == n)
                def _():
                    chunk_in(t)

        step(g, between)

        for n, t in ((10, 2), (11, 3), (12, 1)):

            @pl.when(g == n)
            def _():
                deliver(t)

        return carry

    lax.fori_loop(4, 15, loop, 0)
    score(15, 1)
    weigh(15, 0)
    score(15, 2)
    deliver_last(0)
    weigh(15, 1)
    deliver_last(1)
    weigh(15, 2)
    deliver_last(2)

    for t in (2, 3, 1):
        for ry, rz in TILES[t]:
            part(ry, rz).wait_recv()
    for h in range(GH):
        for ry, rz in TILES[0][1:]:
            part_head(ry, rz, h).wait_recv()
        for rz in range(4):
            row, weights = [], []
            for ry in range(4):
                n = QUERY_SLOT[ry, rz]
                if n < 4:
                    stats = h_recv[n, h, HEAD_DIM:, :].astype(f32)
                    row.append([stats[i : i + 1] for i in range(5)])
                    weights.append(h_recv[n, h, :HEAD_DIM, :])
                else:
                    stats = o_recv[n, GD:, :].astype(f32)
                    row.append([stats[GH * i + h : GH * i + h + 1] for i in range(5)])
                    weights.append(o_recv[n, h * HEAD_DIM : (h + 1) * HEAD_DIM, :])
            tops = [r[0] + r[1] + r[2] for r in row]
            most = jnp.maximum(jnp.maximum(tops[0], tops[1]), jnp.maximum(tops[2], tops[3]))
            total = jnp.exp2(-most)
            weighted = jnp.zeros((HEAD_DIM, ROWS), f32)
            for ry in range(4):
                factor = jnp.exp2(tops[ry] - most)
                total = total + (row[ry][3] + row[ry][4]) * factor
                weighted = weighted + weights[ry].astype(f32) * factor
            rows = slice(h * HEAD_DIM, (h + 1) * HEAD_DIM)
            out_ref[(z + rz) % 4, rows, :] = (weighted / total).astype(bf16)

    for r in (1, 2, 3):
        for copy in (queries_z, keys_z):
            copy(r).wait_send()
    for r in range(4):
        for copy in (keys_up, keys_down, keys_on):
            copy(r).wait_send()
        for rx in range(4):
            keys_core(rx, r).wait_send()
        for ry in (1, 2, 3):
            queries_y(ry, r).wait_send()
    for t in (1, 2, 3):
        for ry, rz in TILES[t]:
            part(ry, rz).wait_send()
    for h in range(GH):
        for ry, rz in TILES[0][1:]:
            part_head(ry, rz, h).wait_send()


def on_device(queries, keys, values, valid, out_weight):
    bf16, f32 = jnp.bfloat16, jnp.float32
    whole = pl.BlockSpec(memory_space=pltpu.VMEM)
    attended = pl.pallas_call(
        kernel,
        out_shape=jax.ShapeDtypeStruct((GROUPS, GD, ROWS), bf16),
        in_specs=[whole] * 4,
        out_specs=whole,
        scratch_shapes=[
            pltpu.VMEM((GROUPS, SHARD, ROWS), bf16),
            pltpu.VMEM((GROUPS, GD, ROWS), bf16),
            pltpu.VMEM((2, 16, SHARD, ROWS), bf16),
            pltpu.VMEM((4, 4, GD, ROWS), bf16),
            pltpu.VMEM((4, 2 * ROWS, 4 * TILE), bf16),
            pltpu.VMEM((GH, 8, 2, HEAD_DIM, TILE), f32),
            pltpu.VMEM((GH, HEAD_DIM + 16, 4 * TILE), f32),
            pltpu.VMEM((GH, 1, 4 * TILE), f32),
            pltpu.VMEM((GH, 1, TILE), f32),
            pltpu.VMEM((GH, 1, TILE), f32),
            pltpu.VMEM((16, TILE), f32),
            pltpu.VMEM((GH, 16, TILE), f32),
            pltpu.VMEM((16, PART, ROWS), bf16),
            pltpu.VMEM((16, PART, ROWS), bf16),
            pltpu.VMEM((4, GH, LAST, ROWS), bf16),
            pltpu.VMEM((4, GH, LAST, ROWS), bf16),
            pltpu.SemaphoreType.DMA((COPIES,)),
            pltpu.SemaphoreType.DMA((COPIES,)),
        ],
        compiler_params=pltpu.CompilerParams(
            collective_id=0, has_side_effects=True, vmem_limit_bytes=56 << 20
        ),
        name="attend",
    )(queries, keys, values, valid.reshape(1, ROWS))
    mixed = lax.dot_general(
        attended.reshape(HEADS * HEAD_DIM, ROWS),
        out_weight,
        (((0,), (0,)), ((), ())),
        preferred_element_type=f32,
    )
    return mixed.astype(bf16)


def solution(mesh):
    return jax.shard_map(
        on_device,
        mesh=mesh,
        in_specs=(
            P(("blk", "inner"), None),
            P(("blk", "inner"), None),
            P(("blk", "inner"), None),
            P(("blk", "inner")),
            P(),
        ),
        out_specs=P(("blk", "inner"), None),
        check_vma=False,
    )
```

```python
import jax
import jax.numpy as jnp
from jax import lax
from jax.experimental import pallas as pl
from jax.experimental.pallas import tpu as pltpu
from jax.sharding import PartitionSpec as P

HEADS = 12
HEAD_DIM = 64
GROUPS = 4
GH = HEADS // GROUPS
ROWS = 128
GD = GH * HEAD_DIM
TILE = 4 * ROWS
KROWS = ROWS + HEAD_DIM
SHARD = KROWS + GD + 16
PART = GD + 16
LAST = HEAD_DIM + 16
LOG2E = 1.4426950408889634
MESH = pl.DeviceIdType.MESH

KA, QA, QY, KX, KF, KC, OP, OH = 0, 4, 8, 24, 32, 36, 52, 68
COPIES = OH + 12

CHUNKS = (
    ((0, 0), (0, 1), (1, 0), (0, 3)),
    ((3, 0), (1, 1), (3, 1), (0, 2)),
    ((1, 3), (3, 3), (1, 2), (3, 2)),
    ((2, 0), (2, 1), (2, 3), (2, 2)),
)
KEY_SLOT = {owner: 4 * t + n for t, chunk in enumerate(CHUNKS) for n, owner in enumerate(chunk)}
TILES = (
    ((0, 0), (0, 1), (0, 3), (1, 0)),
    ((0, 2), (1, 1), (3, 0), (2, 0)),
    ((2, 1), (2, 3), (2, 2), (3, 2)),
    ((3, 1), (1, 3), (3, 3), (1, 2)),
)
QUERY_SLOT = {owner: 4 * t + n for t, tile in enumerate(TILES) for n, owner in enumerate(tile)}
CHUNK_AT = (0, 0, 0, 1, 1, 0, 1, 2, 2, 2, 3, 3, 3, 1, 2, 3)
TILE_AT = (0, 1, 3, 3, 1, 2, 2, 2, 3, 1, 2, 3, 1, 0, 0, 0)


def lookup(table, g):
    if isinstance(g, int):
        return table[g]
    packed = sum(n << 2 * i for i, n in enumerate(table[4:]))
    return lax.shift_right_logical(jnp.int32(packed), 2 * (g - 4)) % 4


def kernel(
    q_ref, k_ref, v_ref, valid_ref, out_ref,
    kv_src, q_src, kv, qb, qs, sb, acc, top, shrink, cur, stat, stat_last, o_send, o_recv, h_send, h_recv,
    send_sem, recv_sem,
):
    bf16, f32 = jnp.bfloat16, jnp.float32
    blk = lax.axis_index("blk")
    inner = lax.axis_index("inner")
    y, x, c = blk % 4, inner // 4, inner % 2
    z = (inner // 2 % 2) * 2 + blk // 4

    def at(dx=0, dy=0, dz=0, dc=0):
        tx, ty, tz, tc = (x + dx) % 4, (y + dy) % 4, (z + dz) % 4, (c + dc) % 2
        return ((tz % 2) * 4 + ty, tx * 4 + (tz // 2) * 2 + tc)

    def send(src, dst, number, device):
        return pltpu.make_async_remote_copy(
            src_ref=src, dst_ref=dst, send_sem=send_sem.at[number], recv_sem=recv_sem.at[number],
            device_id=device, device_id_type=MESH,
        )

    def keys(cc, rx, rz):
        return kv.at[cc, KEY_SLOT[rx, rz]]

    def keys_z(r):
        return send(kv_src.at[(z + r) % 4], keys(0, 0, r), KA + r, at(dz=r))

    def queries_z(r):
        return send(q_src.at[(z + r) % 4], qb.at[0, r], QA + r, at(dz=r))

    def queries_y(ry, rz):
        return send(qb.at[0, rz], qb.at[ry, rz], QY + 4 * ry + rz, at(dy=ry))

    def keys_up(rz):
        return send(keys(0, 0, rz), keys(0, 1, rz), KX + rz, at(dx=1))

    def keys_down(rz):
        return send(keys(0, 0, rz), keys(0, 3, rz), KX + 4 + rz, at(dx=3))

    def keys_on(rz):
        if rz in (0, 3):
            return send(keys(0, 1, rz), keys(0, 2, rz), KF + rz, at(dx=1))
        return send(keys(0, 3, rz), keys(0, 2, rz), KF + rz, at(dx=3))

    def keys_core(rx, rz):
        return send(keys(0, rx, rz), keys(1, rx, rz), KC + KEY_SLOT[rx, rz], at(dc=1))

    def part(ry, rz):
        n = QUERY_SLOT[ry, rz]
        return send(o_send.at[n], o_recv.at[n], OP + n, at(dy=4 - ry, dz=4 - rz))

    def part_head(ry, rz, h):
        n = QUERY_SLOT[ry, rz]
        return send(h_send.at[n, h], h_recv.at[n, h], OH + 4 * h + n, at(dy=4 - ry, dz=4 - rz))

    barrier = pltpu.get_barrier_semaphore()
    partners = [at(dc=1), at(dx=1), at(dx=3)]
    partners += [at(dy=ry, dz=rz) for ry in range(4) for rz in range(4) if ry or rz]
    for device in partners:
        pl.semaphore_signal(barrier, inc=1, device_id=device, device_id_type=MESH)

    turned = q_ref[...].T
    for g in range(GROUPS):
        q_src[g] = turned[g * GD : (g + 1) * GD]
    qb[0, 0] = q_src[z]

    pl.semaphore_wait(barrier, len(partners))
    for r in (1, 3, 2):
        queries_z(r).start()
    for r in (1, 3, 2):
        queries_y(r, 0).start()

    flag_row = jnp.where(valid_ref[...] > 0, 1.0, 0.0).astype(f32)
    flag_square = jnp.broadcast_to(flag_row, (ROWS, ROWS))
    key_flags = flag_square.T.astype(bf16)
    value_flags = flag_square[:1].astype(bf16)
    first_row = lax.broadcasted_iota(jnp.int32, (16, ROWS), 0) == 0
    flag_rows = jnp.where(first_row, jnp.broadcast_to(flag_row, (16, ROWS)), 0.0).astype(bf16)
    turned = v_ref[...].T
    for g in range(GROUPS):
        kv_src[g, :ROWS, :] = k_ref[:, g * GD : g * GD + ROWS] * key_flags
        third = k_ref[:, g * GD + ROWS : (g + 1) * GD] * key_flags[:, :HEAD_DIM]
        kv_src[g, ROWS:KROWS, :] = jnp.concatenate([third[:HEAD_DIM], third[HEAD_DIM:]], axis=1)
        kv_src[g, KROWS : KROWS + GD, :] = turned[g * GD : (g + 1) * GD] * value_flags
        kv_src[g, KROWS + GD :, :] = flag_rows
    kv[0, KEY_SLOT[0, 0]] = kv_src[z]
    for r in (1, 3):
        keys_z(r).start()
    keys_up(0).start()
    keys_down(0).start()
    keys_core(0, 0).start()
    qs[...] = jnp.zeros_like(qs)
    acc[...] = jnp.zeros_like(acc)
    top[...] = jnp.zeros_like(top)
    stat[...] = jnp.zeros_like(stat)
    stat_last[...] = jnp.zeros_like(stat_last)

    def prepare(t):
        for ry, rz in TILES[t]:
            columns = pl.ds(QUERY_SLOT[ry, rz] * ROWS, ROWS)
            scaled = qb[ry, rz].astype(f32) * (LOG2E * HEAD_DIM**-0.5)
            high = scaled.astype(bf16)
            low = (scaled - high.astype(f32)).astype(bf16)
            for n, h, at_row in ((0, 0, 0), (1, 1, 1), (2, 2, 0), (3, 2, 1)):
                rows = slice(h * HEAD_DIM, (h + 1) * HEAD_DIM)
                qs[n, at_row * HEAD_DIM : (at_row + 1) * HEAD_DIM, columns] = high[rows]
                qs[n, ROWS + at_row * HEAD_DIM : ROWS + (at_row + 1) * HEAD_DIM, columns] = low[
                    rows
                ]

    for r in (1, 3, 2):
        queries_z(r).wait_recv()
        queries_y(1, r).start()
        queries_y(3, r).start()
    queries_y(1, 0).wait_recv()
    prepare(0)
    for r in (1, 3, 2):
        queries_y(2, r).start()

    def keys_in(copy, rx, rz):
        copy(rz).wait_recv()
        keys_core(rx, rz).start()

    def chunk_in(t):
        for rx, rz in CHUNKS[t]:
            keys_core(rx, rz).wait_recv()

    for r in (1, 3):
        keys_in(keys_z, 0, r)
        keys_up(r).start()
        keys_down(r).start()
    keys_z(2).start()
    keys_in(keys_up, 1, 0)
    keys_on(0).start()
    keys_in(keys_down, 3, 0)
    chunk_in(0)

    def tile(ry):
        return pl.ds(pl.multiple_of(ry * TILE, TILE), TILE)

    def score(g, h):
        chunk = 4 * lookup(CHUNK_AT, g)
        columns = tile(lookup(TILE_AT, g))
        rows = slice(0, ROWS) if h < 2 else slice(ROWS, KROWS)
        keys = jnp.concatenate(
            [kv[cc, chunk + n, rows, :] for cc in range(2) for n in range(4)], axis=0
        )
        keys = jnp.concatenate([keys, keys], axis=1)
        if h < 2:
            s = jnp.dot(keys, qs[h, :, columns], preferred_element_type=f32)
            sb[h] = s.reshape(8, 2, HEAD_DIM, TILE)
            most = jnp.max(s, axis=0, keepdims=True)
        else:
            sa = jnp.dot(keys, qs[2, :, columns], preferred_element_type=f32)
            sb[h, :, 0] = sa.reshape(8, HEAD_DIM, TILE)
            sc = jnp.dot(keys, qs[3, :, columns], preferred_element_type=f32)
            sb[h, :, 1] = sc.reshape(8, HEAD_DIM, TILE)
            most = jnp.maximum(
                jnp.max(sa, axis=0, keepdims=True), jnp.max(sc, axis=0, keepdims=True)
            )
        old = top[h, :, columns]
        new = jnp.maximum(old, most)
        shrink[h] = jnp.exp2(old - new)
        top[h, :, columns] = new
        cur[h] = new

    def weigh(g, h):
        chunk = 4 * lookup(CHUNK_AT, g)
        columns = tile(lookup(TILE_AT, g))
        chances = jnp.exp2(sb[h].reshape(8 * ROWS, TILE) - cur[h]).astype(bf16)
        first = KROWS + h * HEAD_DIM
        values = jnp.concatenate(
            [
                jnp.concatenate(
                    [
                        kv[cc, chunk + n, first : first + HEAD_DIM, :],
                        kv[cc, chunk + n, KROWS + GD :, :],
                    ],
                    axis=0,
                )
                for cc in range(2)
                for n in range(4)
            ],
            axis=1,
        )
        acc[h, :, columns] = acc[h, :, columns] * shrink[h] + jnp.dot(
            values, chances, preferred_element_type=f32
        )

    def step(g, between=None):
        score(g, 1)
        weigh(g, 0)
        score(g, 2)
        weigh(g, 1)
        if between is not None:
            between()
        score(g + 1, 0)
        weigh(g, 2)

    def pieces(store, at_row, value, n):
        for i in range(n):
            piece = value.astype(bf16).astype(f32)
            store[at_row(i), :] = piece
            value = value - piece

    def deliver(t):
        columns = pl.ds(t * TILE, TILE)
        for h in range(GH):
            pieces(stat, lambda i: pl.ds(GH * i + h, 1), top[h, :, columns], 3)
            total = acc[h, HEAD_DIM : HEAD_DIM + 1, columns]
            pieces(stat, lambda i: pl.ds(GH * (i + 3) + h, 1), total, 2)
        for n, (ry, rz) in enumerate(TILES[t]):
            slot = 4 * t + n
            for h in range(GH):
                rows = pl.ds(h * HEAD_DIM, HEAD_DIM)
                o_send[slot, rows, :] = acc[h, :HEAD_DIM, pl.ds(slot * ROWS, ROWS)].astype(bf16)
            o_send[slot, GD:, :] = stat[:, n * ROWS : (n + 1) * ROWS].astype(bf16)
            part(ry, rz).start()

    def deliver_last(h):
        columns = pl.ds(0, TILE)
        store = stat_last.at[h]
        pieces(store, lambda i: pl.ds(i, 1), top[h, :, columns], 3)
        pieces(store, lambda i: pl.ds(i + 3, 1), acc[h, HEAD_DIM : HEAD_DIM + 1, columns], 2)
        for n in (1, 2, 3, 0):
            to = h_send if n else h_recv
            to[n, h, :HEAD_DIM, :] = acc[h, :HEAD_DIM, pl.ds(n * ROWS, ROWS)].astype(bf16)
            to[n, h, HEAD_DIM:, :] = stat_last[h, :, n * ROWS : (n + 1) * ROWS].astype(bf16)
            if n:
                part_head(*TILES[0][n], h).start()

    def queries_in(t):
        for ry, rz in TILES[t]:
            if ry:
                queries_y(ry, rz).wait_recv()
        prepare(t)

    score(0, 0)
    step(0, lambda: queries_in(1))
    step(1, lambda: queries_in(3))
    keys_in(keys_z, 0, 2)
    keys_in(keys_down, 3, 1)
    keys_in(keys_up, 1, 1)
    keys_up(2).start()
    keys_down(2).start()
    keys_on(1).start()
    step(2, lambda: chunk_in(1))
    step(3)
    keys_in(keys_up, 1, 3)
    keys_on(3).start()
    keys_in(keys_down, 3, 3)
    step(4, lambda: queries_in(2))

    def loop(g, carry):
        @pl.when(g == 5)
        def _():
            keys_in(keys_down, 3, 2)
            keys_on(2).start()
            keys_in(keys_up, 1, 2)

        @pl.when(g == 6)
        def _():
            chunk_in(2)

        @pl.when(g == 7)
        def _():
            for rz in (0, 1, 3):
                keys_in(keys_on, 2, rz)

        @pl.when(g == 8)
        def _():
            keys_in(keys_on, 2, 2)

        @pl.when(g == 9)
        def _():
            chunk_in(3)

        step(g)

        for n, t in ((10, 2), (11, 3), (12, 1)):

            @pl.when(g == n)
            def _():
                deliver(t)

        return carry

    lax.fori_loop(5, 15, loop, 0)
    score(15, 1)
    weigh(15, 0)
    score(15, 2)
    deliver_last(0)
    weigh(15, 1)
    deliver_last(1)
    weigh(15, 2)
    deliver_last(2)

    for t in (2, 3, 1):
        for ry, rz in TILES[t]:
            part(ry, rz).wait_recv()
    for h in range(GH):
        for ry, rz in TILES[0][1:]:
            part_head(ry, rz, h).wait_recv()
        for rz in range(4):
            row, weights = [], []
            for ry in range(4):
                n = QUERY_SLOT[ry, rz]
                if n < 4:
                    stats = h_recv[n, h, HEAD_DIM:, :].astype(f32)
                    row.append([stats[i : i + 1] for i in range(5)])
                    weights.append(h_recv[n, h, :HEAD_DIM, :])
                else:
                    stats = o_recv[n, GD:, :].astype(f32)
                    row.append([stats[GH * i + h : GH * i + h + 1] for i in range(5)])
                    weights.append(o_recv[n, h * HEAD_DIM : (h + 1) * HEAD_DIM, :])
            tops = [r[0] + r[1] + r[2] for r in row]
            most = jnp.maximum(jnp.maximum(tops[0], tops[1]), jnp.maximum(tops[2], tops[3]))
            total = jnp.exp2(-most)
            weighted = jnp.zeros((HEAD_DIM, ROWS), f32)
            for ry in range(4):
                factor = jnp.exp2(tops[ry] - most)
                total = total + (row[ry][3] + row[ry][4]) * factor
                weighted = weighted + weights[ry].astype(f32) * factor
            rows = slice(h * HEAD_DIM, (h + 1) * HEAD_DIM)
            out_ref[(z + rz) % 4, rows, :] = (weighted / total).astype(bf16)

    for r in (1, 2, 3):
        for copy in (queries_z, keys_z):
            copy(r).wait_send()
    for r in range(4):
        for copy in (keys_up, keys_down, keys_on):
            copy(r).wait_send()
        for rx in range(4):
            keys_core(rx, r).wait_send()
        for ry in (1, 2, 3):
            queries_y(ry, r).wait_send()
    for t in (1, 2, 3):
        for ry, rz in TILES[t]:
            part(ry, rz).wait_send()
    for h in range(GH):
        for ry, rz in TILES[0][1:]:
            part_head(ry, rz, h).wait_send()


def on_device(queries, keys, values, valid, out_weight):
    bf16, f32 = jnp.bfloat16, jnp.float32
    whole = pl.BlockSpec(memory_space=pltpu.VMEM)
    attended = pl.pallas_call(
        kernel,
        out_shape=jax.ShapeDtypeStruct((GROUPS, GD, ROWS), bf16),
        in_specs=[whole] * 4,
        out_specs=whole,
        scratch_shapes=[
            pltpu.VMEM((GROUPS, SHARD, ROWS), bf16),
            pltpu.VMEM((GROUPS, GD, ROWS), bf16),
            pltpu.VMEM((2, 16, SHARD, ROWS), bf16),
            pltpu.VMEM((4, 4, GD, ROWS), bf16),
            pltpu.VMEM((4, 2 * ROWS, 4 * TILE), bf16),
            pltpu.VMEM((GH, 8, 2, HEAD_DIM, TILE), f32),
            pltpu.VMEM((GH, HEAD_DIM + 16, 4 * TILE), f32),
            pltpu.VMEM((GH, 1, 4 * TILE), f32),
            pltpu.VMEM((GH, 1, TILE), f32),
            pltpu.VMEM((GH, 1, TILE), f32),
            pltpu.VMEM((16, TILE), f32),
            pltpu.VMEM((GH, 16, TILE), f32),
            pltpu.VMEM((16, PART, ROWS), bf16),
            pltpu.VMEM((16, PART, ROWS), bf16),
            pltpu.VMEM((4, GH, LAST, ROWS), bf16),
            pltpu.VMEM((4, GH, LAST, ROWS), bf16),
            pltpu.SemaphoreType.DMA((COPIES,)),
            pltpu.SemaphoreType.DMA((COPIES,)),
        ],
        compiler_params=pltpu.CompilerParams(
            collective_id=0, has_side_effects=True, vmem_limit_bytes=56 << 20
        ),
        name="attend",
    )(queries, keys, values, valid.reshape(1, ROWS))
    mixed = lax.dot_general(
        attended.reshape(HEADS * HEAD_DIM, ROWS),
        out_weight,
        (((0,), (0,)), ((), ())),
        preferred_element_type=f32,
    )
    return mixed.astype(bf16)


def solution(mesh):
    return jax.shard_map(
        on_device,
        mesh=mesh,
        in_specs=(
            P(("blk", "inner"), None),
            P(("blk", "inner"), None),
            P(("blk", "inner"), None),
            P(("blk", "inner")),
            P(),
        ),
        out_specs=P(("blk", "inner"), None),
        check_vma=False,
    )
```

```python
import jax
import jax.numpy as jnp
from jax import lax
from jax.experimental import pallas as pl
from jax.experimental.pallas import tpu as pltpu
from jax.sharding import PartitionSpec as P

HEADS = 12
HEAD_DIM = 64
GROUPS = 4
GH = HEADS // GROUPS
ROWS = 128
GD = GH * HEAD_DIM
TILE = 4 * ROWS
KROWS = ROWS + HEAD_DIM
SHARD = KROWS + GD + 16
PART = GD + 16
LAST = HEAD_DIM + 16
LOG2E = 1.4426950408889634
MESH = pl.DeviceIdType.MESH

KA, QA, QY, KX, KF, KC, OP, OH = 0, 4, 8, 24, 32, 36, 52, 68
COPIES = OH + 12

CHUNKS = (
    ((0, 0), (0, 1), (1, 0), (0, 3)),
    ((3, 0), (1, 1), (3, 1), (0, 2)),
    ((1, 3), (3, 3), (1, 2), (3, 2)),
    ((2, 0), (2, 1), (2, 3), (2, 2)),
)
KEY_SLOT = {owner: 4 * t + n for t, chunk in enumerate(CHUNKS) for n, owner in enumerate(chunk)}
TILES = (
    ((0, 0), (0, 1), (0, 3), (1, 0)),
    ((0, 2), (1, 1), (3, 0), (2, 0)),
    ((2, 1), (2, 3), (2, 2), (3, 2)),
    ((3, 1), (1, 3), (3, 3), (1, 2)),
)
QUERY_SLOT = {owner: 4 * t + n for t, tile in enumerate(TILES) for n, owner in enumerate(tile)}
CHUNK_AT = (0, 0, 0, 1, 1, 0, 1, 2, 2, 3, 3, 2, 3, 1, 2, 3)
TILE_AT = (0, 1, 3, 3, 1, 2, 2, 2, 3, 2, 3, 1, 1, 0, 0, 0)


def lookup(table, g):
    if isinstance(g, int):
        return table[g]
    packed = sum(n << 2 * i for i, n in enumerate(table[4:]))
    return lax.shift_right_logical(jnp.int32(packed), 2 * (g - 4)) % 4


def kernel(
    q_ref, k_ref, v_ref, valid_ref, out_ref,
    kv_src, q_src, kv, qb, qs, sb, acc, top, shrink, cur, stat, stat_last, o_send, o_recv, h_send, h_recv,
    send_sem, recv_sem,
):
    bf16, f32 = jnp.bfloat16, jnp.float32
    blk = lax.axis_index("blk")
    inner = lax.axis_index("inner")
    y, x, c = blk % 4, inner // 4, inner % 2
    z = (inner // 2 % 2) * 2 + blk // 4

    def at(dx=0, dy=0, dz=0, dc=0):
        tx, ty, tz, tc = (x + dx) % 4, (y + dy) % 4, (z + dz) % 4, (c + dc) % 2
        return ((tz % 2) * 4 + ty, tx * 4 + (tz // 2) * 2 + tc)

    def send(src, dst, number, device):
        return pltpu.make_async_remote_copy(
            src_ref=src, dst_ref=dst, send_sem=send_sem.at[number], recv_sem=recv_sem.at[number],
            device_id=device, device_id_type=MESH,
        )

    def keys(cc, rx, rz):
        return kv.at[cc, KEY_SLOT[rx, rz]]

    def keys_z(r):
        return send(kv_src.at[(z + r) % 4], keys(0, 0, r), KA + r, at(dz=r))

    def queries_z(r):
        return send(q_src.at[(z + r) % 4], qb.at[0, r], QA + r, at(dz=r))

    def queries_y(ry, rz):
        return send(qb.at[0, rz], qb.at[ry, rz], QY + 4 * ry + rz, at(dy=ry))

    def keys_up(rz):
        return send(keys(0, 0, rz), keys(0, 1, rz), KX + rz, at(dx=1))

    def keys_down(rz):
        return send(keys(0, 0, rz), keys(0, 3, rz), KX + 4 + rz, at(dx=3))

    def keys_on(rz):
        if rz in (0, 3):
            return send(keys(0, 1, rz), keys(0, 2, rz), KF + rz, at(dx=1))
        return send(keys(0, 3, rz), keys(0, 2, rz), KF + rz, at(dx=3))

    def keys_core(rx, rz):
        return send(keys(0, rx, rz), keys(1, rx, rz), KC + KEY_SLOT[rx, rz], at(dc=1))

    def part(ry, rz):
        n = QUERY_SLOT[ry, rz]
        return send(o_send.at[n], o_recv.at[n], OP + n, at(dy=4 - ry, dz=4 - rz))

    def part_head(ry, rz, h):
        n = QUERY_SLOT[ry, rz]
        return send(h_send.at[n, h], h_recv.at[n, h], OH + 4 * h + n, at(dy=4 - ry, dz=4 - rz))

    barrier = pltpu.get_barrier_semaphore()
    partners = [at(dc=1), at(dx=1), at(dx=3)]
    partners += [at(dy=ry, dz=rz) for ry in range(4) for rz in range(4) if ry or rz]
    for device in partners:
        pl.semaphore_signal(barrier, inc=1, device_id=device, device_id_type=MESH)

    turned = q_ref[...].T
    for g in range(GROUPS):
        q_src[g] = turned[g * GD : (g + 1) * GD]
    qb[0, 0] = q_src[z]

    pl.semaphore_wait(barrier, len(partners))
    for r in (1, 3, 2):
        queries_z(r).start()
    for r in (1, 3, 2):
        queries_y(r, 0).start()

    flag_row = jnp.where(valid_ref[...] > 0, 1.0, 0.0).astype(f32)
    flag_square = jnp.broadcast_to(flag_row, (ROWS, ROWS))
    key_flags = flag_square.T.astype(bf16)
    value_flags = flag_square[:1].astype(bf16)
    first_row = lax.broadcasted_iota(jnp.int32, (16, ROWS), 0) == 0
    flag_rows = jnp.where(first_row, jnp.broadcast_to(flag_row, (16, ROWS)), 0.0).astype(bf16)
    turned = v_ref[...].T
    for g in range(GROUPS):
        kv_src[g, :ROWS, :] = k_ref[:, g * GD : g * GD + ROWS] * key_flags
        third = k_ref[:, g * GD + ROWS : (g + 1) * GD] * key_flags[:, :HEAD_DIM]
        kv_src[g, ROWS:KROWS, :] = jnp.concatenate([third[:HEAD_DIM], third[HEAD_DIM:]], axis=1)
        kv_src[g, KROWS : KROWS + GD, :] = turned[g * GD : (g + 1) * GD] * value_flags
        kv_src[g, KROWS + GD :, :] = flag_rows
    kv[0, KEY_SLOT[0, 0]] = kv_src[z]
    for r in (1, 3):
        keys_z(r).start()
    keys_up(0).start()
    keys_down(0).start()
    keys_core(0, 0).start()
    qs[...] = jnp.zeros_like(qs)
    acc[...] = jnp.zeros_like(acc)
    top[...] = jnp.zeros_like(top)
    stat[...] = jnp.zeros_like(stat)
    stat_last[...] = jnp.zeros_like(stat_last)

    def prepare(t):
        for ry, rz in TILES[t]:
            columns = pl.ds(QUERY_SLOT[ry, rz] * ROWS, ROWS)
            scaled = qb[ry, rz].astype(f32) * (LOG2E * HEAD_DIM**-0.5)
            high = scaled.astype(bf16)
            low = (scaled - high.astype(f32)).astype(bf16)
            for n, h, at_row in ((0, 0, 0), (1, 1, 1), (2, 2, 0), (3, 2, 1)):
                rows = slice(h * HEAD_DIM, (h + 1) * HEAD_DIM)
                qs[n, at_row * HEAD_DIM : (at_row + 1) * HEAD_DIM, columns] = high[rows]
                qs[n, ROWS + at_row * HEAD_DIM : ROWS + (at_row + 1) * HEAD_DIM, columns] = low[
                    rows
                ]

    for r in (1, 3, 2):
        queries_z(r).wait_recv()
        queries_y(1, r).start()
        queries_y(3, r).start()
    queries_y(1, 0).wait_recv()
    prepare(0)
    for r in (1, 3, 2):
        queries_y(2, r).start()

    def keys_in(copy, rx, rz):
        copy(rz).wait_recv()
        keys_core(rx, rz).start()

    def chunk_in(t):
        for rx, rz in CHUNKS[t]:
            keys_core(rx, rz).wait_recv()

    for r in (1, 3):
        keys_in(keys_z, 0, r)
        keys_up(r).start()
        keys_down(r).start()
    keys_z(2).start()
    keys_in(keys_up, 1, 0)
    keys_on(0).start()
    keys_in(keys_down, 3, 0)
    chunk_in(0)

    def tile(ry):
        return pl.ds(pl.multiple_of(ry * TILE, TILE), TILE)

    def score(g, h):
        chunk = 4 * lookup(CHUNK_AT, g)
        columns = tile(lookup(TILE_AT, g))
        rows = slice(0, ROWS) if h < 2 else slice(ROWS, KROWS)
        keys = jnp.concatenate(
            [kv[cc, chunk + n, rows, :] for cc in range(2) for n in range(4)], axis=0
        )
        keys = jnp.concatenate([keys, keys], axis=1)
        if h < 2:
            s = jnp.dot(keys, qs[h, :, columns], preferred_element_type=f32)
            sb[h] = s.reshape(8, 2, HEAD_DIM, TILE)
            most = jnp.max(s, axis=0, keepdims=True)
        else:
            sa = jnp.dot(keys, qs[2, :, columns], preferred_element_type=f32)
            sb[h, :, 0] = sa.reshape(8, HEAD_DIM, TILE)
            sc = jnp.dot(keys, qs[3, :, columns], preferred_element_type=f32)
            sb[h, :, 1] = sc.reshape(8, HEAD_DIM, TILE)
            most = jnp.maximum(
                jnp.max(sa, axis=0, keepdims=True), jnp.max(sc, axis=0, keepdims=True)
            )
        old = top[h, :, columns]
        new = jnp.maximum(old, most)
        shrink[h] = jnp.exp2(old - new)
        top[h, :, columns] = new
        cur[h] = new

    def weigh(g, h):
        chunk = 4 * lookup(CHUNK_AT, g)
        columns = tile(lookup(TILE_AT, g))
        chances = jnp.exp2(sb[h].reshape(8 * ROWS, TILE) - cur[h]).astype(bf16)
        first = KROWS + h * HEAD_DIM
        values = jnp.concatenate(
            [
                jnp.concatenate(
                    [
                        kv[cc, chunk + n, first : first + HEAD_DIM, :],
                        kv[cc, chunk + n, KROWS + GD :, :],
                    ],
                    axis=0,
                )
                for cc in range(2)
                for n in range(4)
            ],
            axis=1,
        )
        acc[h, :, columns] = acc[h, :, columns] * shrink[h] + jnp.dot(
            values, chances, preferred_element_type=f32
        )

    def step(g, between=None):
        score(g, 1)
        weigh(g, 0)
        score(g, 2)
        weigh(g, 1)
        if between is not None:
            between()
        score(g + 1, 0)
        weigh(g, 2)

    def pieces(store, at_row, value, n):
        for i in range(n):
            piece = value.astype(bf16).astype(f32)
            store[at_row(i), :] = piece
            value = value - piece

    def deliver(t):
        columns = pl.ds(t * TILE, TILE)
        for h in range(GH):
            pieces(stat, lambda i: pl.ds(GH * i + h, 1), top[h, :, columns], 3)
            total = acc[h, HEAD_DIM : HEAD_DIM + 1, columns]
            pieces(stat, lambda i: pl.ds(GH * (i + 3) + h, 1), total, 2)
        for n, (ry, rz) in enumerate(TILES[t]):
            slot = 4 * t + n
            for h in range(GH):
                rows = pl.ds(h * HEAD_DIM, HEAD_DIM)
                o_send[slot, rows, :] = acc[h, :HEAD_DIM, pl.ds(slot * ROWS, ROWS)].astype(bf16)
            o_send[slot, GD:, :] = stat[:, n * ROWS : (n + 1) * ROWS].astype(bf16)
            part(ry, rz).start()

    def deliver_last(h):
        columns = pl.ds(0, TILE)
        store = stat_last.at[h]
        pieces(store, lambda i: pl.ds(i, 1), top[h, :, columns], 3)
        pieces(store, lambda i: pl.ds(i + 3, 1), acc[h, HEAD_DIM : HEAD_DIM + 1, columns], 2)
        for n in (1, 2, 3, 0):
            to = h_send if n else h_recv
            to[n, h, :HEAD_DIM, :] = acc[h, :HEAD_DIM, pl.ds(n * ROWS, ROWS)].astype(bf16)
            to[n, h, HEAD_DIM:, :] = stat_last[h, :, n * ROWS : (n + 1) * ROWS].astype(bf16)
            if n:
                part_head(*TILES[0][n], h).start()

    def queries_in(t):
        for ry, rz in TILES[t]:
            if ry:
                queries_y(ry, rz).wait_recv()
        prepare(t)

    score(0, 0)
    step(0, lambda: queries_in(1))
    step(1, lambda: queries_in(3))
    keys_in(keys_z, 0, 2)
    keys_in(keys_down, 3, 1)
    keys_in(keys_up, 1, 1)
    keys_up(2).start()
    keys_down(2).start()
    keys_on(1).start()
    step(2, lambda: chunk_in(1))
    step(3)
    keys_in(keys_up, 1, 3)
    keys_on(3).start()
    keys_in(keys_down, 3, 3)
    step(4, lambda: queries_in(2))

    def loop(g, carry):
        @pl.when(g == 5)
        def _():
            keys_in(keys_down, 3, 2)
            keys_on(2).start()
            keys_in(keys_up, 1, 2)

        @pl.when(g == 6)
        def _():
            chunk_in(2)

        @pl.when(g == 7)
        def _():
            for rz in (0, 1, 3, 2):
                keys_in(keys_on, 2, rz)

        @pl.when(g == 8)
        def _():
            chunk_in(3)

        step(g)

        for n, t in ((9, 2), (10, 3), (12, 1)):

            @pl.when(g == n)
            def _():
                deliver(t)

        return carry

    lax.fori_loop(5, 15, loop, 0)
    score(15, 1)
    weigh(15, 0)
    score(15, 2)
    deliver_last(0)
    weigh(15, 1)
    deliver_last(1)
    weigh(15, 2)
    deliver_last(2)

    for t in (2, 3, 1):
        for ry, rz in TILES[t]:
            part(ry, rz).wait_recv()
    for h in range(GH):
        for ry, rz in TILES[0][1:]:
            part_head(ry, rz, h).wait_recv()
        for rz in range(4):
            row, weights = [], []
            for ry in range(4):
                n = QUERY_SLOT[ry, rz]
                if n < 4:
                    stats = h_recv[n, h, HEAD_DIM:, :].astype(f32)
                    row.append([stats[i : i + 1] for i in range(5)])
                    weights.append(h_recv[n, h, :HEAD_DIM, :])
                else:
                    stats = o_recv[n, GD:, :].astype(f32)
                    row.append([stats[GH * i + h : GH * i + h + 1] for i in range(5)])
                    weights.append(o_recv[n, h * HEAD_DIM : (h + 1) * HEAD_DIM, :])
            tops = [r[0] + r[1] + r[2] for r in row]
            most = jnp.maximum(jnp.maximum(tops[0], tops[1]), jnp.maximum(tops[2], tops[3]))
            total = jnp.exp2(-most)
            weighted = jnp.zeros((HEAD_DIM, ROWS), f32)
            for ry in range(4):
                factor = jnp.exp2(tops[ry] - most)
                total = total + (row[ry][3] + row[ry][4]) * factor
                weighted = weighted + weights[ry].astype(f32) * factor
            rows = slice(h * HEAD_DIM, (h + 1) * HEAD_DIM)
            out_ref[(z + rz) % 4, rows, :] = (weighted / total).astype(bf16)

    for r in (1, 2, 3):
        for copy in (queries_z, keys_z):
            copy(r).wait_send()
    for r in range(4):
        for copy in (keys_up, keys_down, keys_on):
            copy(r).wait_send()
        for rx in range(4):
            keys_core(rx, r).wait_send()
        for ry in (1, 2, 3):
            queries_y(ry, r).wait_send()
    for t in (1, 2, 3):
        for ry, rz in TILES[t]:
            part(ry, rz).wait_send()
    for h in range(GH):
        for ry, rz in TILES[0][1:]:
            part_head(ry, rz, h).wait_send()


def on_device(queries, keys, values, valid, out_weight):
    bf16, f32 = jnp.bfloat16, jnp.float32
    whole = pl.BlockSpec(memory_space=pltpu.VMEM)
    attended = pl.pallas_call(
        kernel,
        out_shape=jax.ShapeDtypeStruct((GROUPS, GD, ROWS), bf16),
        in_specs=[whole] * 4,
        out_specs=whole,
        scratch_shapes=[
            pltpu.VMEM((GROUPS, SHARD, ROWS), bf16),
            pltpu.VMEM((GROUPS, GD, ROWS), bf16),
            pltpu.VMEM((2, 16, SHARD, ROWS), bf16),
            pltpu.VMEM((4, 4, GD, ROWS), bf16),
            pltpu.VMEM((4, 2 * ROWS, 4 * TILE), bf16),
            pltpu.VMEM((GH, 8, 2, HEAD_DIM, TILE), f32),
            pltpu.VMEM((GH, HEAD_DIM + 16, 4 * TILE), f32),
            pltpu.VMEM((GH, 1, 4 * TILE), f32),
            pltpu.VMEM((GH, 1, TILE), f32),
            pltpu.VMEM((GH, 1, TILE), f32),
            pltpu.VMEM((16, TILE), f32),
            pltpu.VMEM((GH, 16, TILE), f32),
            pltpu.VMEM((16, PART, ROWS), bf16),
            pltpu.VMEM((16, PART, ROWS), bf16),
            pltpu.VMEM((4, GH, LAST, ROWS), bf16),
            pltpu.VMEM((4, GH, LAST, ROWS), bf16),
            pltpu.SemaphoreType.DMA((COPIES,)),
            pltpu.SemaphoreType.DMA((COPIES,)),
        ],
        compiler_params=pltpu.CompilerParams(
            collective_id=0, has_side_effects=True, vmem_limit_bytes=56 << 20
        ),
        name="attend",
    )(queries, keys, values, valid.reshape(1, ROWS))
    mixed = lax.dot_general(
        attended.reshape(HEADS * HEAD_DIM, ROWS),
        out_weight,
        (((0,), (0,)), ((), ())),
        preferred_element_type=f32,
    )
    return mixed.astype(bf16)


def solution(mesh):
    return jax.shard_map(
        on_device,
        mesh=mesh,
        in_specs=(
            P(("blk", "inner"), None),
            P(("blk", "inner"), None),
            P(("blk", "inner"), None),
            P(("blk", "inner")),
            P(),
        ),
        out_specs=P(("blk", "inner"), None),
        check_vma=False,
    )
```

```python
import jax
import jax.numpy as jnp
from jax import lax
from jax.experimental import pallas as pl
from jax.experimental.pallas import tpu as pltpu
from jax.sharding import PartitionSpec as P

HEADS = 12
HEAD_DIM = 64
GROUPS = 4
GH = HEADS // GROUPS
ROWS = 128
GD = GH * HEAD_DIM
TILE = 4 * ROWS
KROWS = ROWS + HEAD_DIM
SHARD = KROWS + GD + 16
PART = GD + 16
LAST = HEAD_DIM + 16
LOG2E = 1.4426950408889634
MESH = pl.DeviceIdType.MESH

KA, QA, QY, KX, KF, KC, OP, OH = 0, 4, 8, 24, 32, 36, 52, 68
COPIES = OH + 12

CHUNKS = (
    ((0, 0), (0, 1), (1, 0), (0, 3)),
    ((3, 0), (1, 1), (3, 1), (0, 2)),
    ((1, 3), (3, 3), (1, 2), (3, 2)),
    ((2, 0), (2, 1), (2, 3), (2, 2)),
)
KEY_SLOT = {owner: 4 * t + n for t, chunk in enumerate(CHUNKS) for n, owner in enumerate(chunk)}
TILES = (
    ((0, 0), (0, 1), (0, 3), (1, 0)),
    ((0, 2), (1, 1), (3, 0), (2, 0)),
    ((2, 1), (2, 3), (2, 2), (3, 2)),
    ((3, 1), (1, 3), (3, 3), (1, 2)),
)
QUERY_SLOT = {owner: 4 * t + n for t, tile in enumerate(TILES) for n, owner in enumerate(tile)}
CHUNK_AT = (0, 0, 0, 1, 1, 0, 1, 2, 2, 3, 3, 2, 3, 1, 2, 3)
TILE_AT = (0, 1, 3, 3, 1, 2, 2, 2, 3, 2, 3, 1, 1, 0, 0, 0)


def lookup(table, g):
    if isinstance(g, int):
        return table[g]
    packed = sum(n << 2 * i for i, n in enumerate(table[4:]))
    return lax.shift_right_logical(jnp.int32(packed), 2 * (g - 4)) % 4


def kernel(
    q_ref, k_ref, v_ref, valid_ref, out_ref,
    kv_src, q_src, kv, qb, qs, sb, acc, top, shrink, cur, stat, stat_last, o_send, o_recv, h_send, h_recv,
    send_sem, recv_sem,
):
    bf16, f32 = jnp.bfloat16, jnp.float32
    blk = lax.axis_index("blk")
    inner = lax.axis_index("inner")
    y, x, c = blk % 4, inner // 4, inner % 2
    z = (inner // 2 % 2) * 2 + blk // 4

    def at(dx=0, dy=0, dz=0, dc=0):
        tx, ty, tz, tc = (x + dx) % 4, (y + dy) % 4, (z + dz) % 4, (c + dc) % 2
        return ((tz % 2) * 4 + ty, tx * 4 + (tz // 2) * 2 + tc)

    def send(src, dst, number, device):
        return pltpu.make_async_remote_copy(
            src_ref=src, dst_ref=dst, send_sem=send_sem.at[number], recv_sem=recv_sem.at[number],
            device_id=device, device_id_type=MESH,
        )

    def keys(cc, rx, rz):
        return kv.at[cc, KEY_SLOT[rx, rz]]

    def keys_z(r):
        return send(kv_src.at[(z + r) % 4], keys(0, 0, r), KA + r, at(dz=r))

    def queries_z(r):
        return send(q_src.at[(z + r) % 4], qb.at[0, r], QA + r, at(dz=r))

    def queries_y(ry, rz):
        return send(qb.at[0, rz], qb.at[ry, rz], QY + 4 * ry + rz, at(dy=ry))

    def keys_up(rz):
        return send(keys(0, 0, rz), keys(0, 1, rz), KX + rz, at(dx=1))

    def keys_down(rz):
        return send(keys(0, 0, rz), keys(0, 3, rz), KX + 4 + rz, at(dx=3))

    def keys_on(rz):
        if rz in (0, 3):
            return send(keys(0, 1, rz), keys(0, 2, rz), KF + rz, at(dx=1))
        return send(keys(0, 3, rz), keys(0, 2, rz), KF + rz, at(dx=3))

    def keys_core(rx, rz):
        return send(keys(0, rx, rz), keys(1, rx, rz), KC + KEY_SLOT[rx, rz], at(dc=1))

    def part(ry, rz):
        n = QUERY_SLOT[ry, rz]
        return send(o_send.at[n], o_recv.at[n], OP + n, at(dy=4 - ry, dz=4 - rz))

    def part_head(ry, rz, h):
        n = QUERY_SLOT[ry, rz]
        return send(h_send.at[n, h], h_recv.at[n, h], OH + 4 * h + n, at(dy=4 - ry, dz=4 - rz))

    barrier = pltpu.get_barrier_semaphore()
    partners = [at(dc=1), at(dx=1), at(dx=3)]
    partners += [at(dy=ry, dz=rz) for ry in range(4) for rz in range(4) if ry or rz]
    for device in partners:
        pl.semaphore_signal(barrier, inc=1, device_id=device, device_id_type=MESH)

    turned = q_ref[...].T
    for g in range(GROUPS):
        q_src[g] = turned[g * GD : (g + 1) * GD]
    qb[0, 0] = q_src[z]

    pl.semaphore_wait(barrier, len(partners))
    for r in (1, 3, 2):
        queries_z(r).start()
    for r in (1, 3, 2):
        queries_y(r, 0).start()

    flag_row = jnp.where(valid_ref[...] > 0, 1.0, 0.0).astype(f32)
    flag_square = jnp.broadcast_to(flag_row, (ROWS, ROWS))
    key_flags = flag_square.T.astype(bf16)
    value_flags = flag_square[:1].astype(bf16)
    first_row = lax.broadcasted_iota(jnp.int32, (16, ROWS), 0) == 0
    flag_rows = jnp.where(first_row, jnp.broadcast_to(flag_row, (16, ROWS)), 0.0).astype(bf16)
    turned = v_ref[...].T
    for g in range(GROUPS):
        kv_src[g, :ROWS, :] = k_ref[:, g * GD : g * GD + ROWS] * key_flags
        third = k_ref[:, g * GD + ROWS : (g + 1) * GD] * key_flags[:, :HEAD_DIM]
        kv_src[g, ROWS:KROWS, :] = jnp.concatenate([third[:HEAD_DIM], third[HEAD_DIM:]], axis=1)
        kv_src[g, KROWS : KROWS + GD, :] = turned[g * GD : (g + 1) * GD] * value_flags
        kv_src[g, KROWS + GD :, :] = flag_rows
    kv[0, KEY_SLOT[0, 0]] = kv_src[z]
    for r in (1, 3):
        keys_z(r).start()
    keys_up(0).start()
    keys_down(0).start()
    keys_core(0, 0).start()
    qs[...] = jnp.zeros_like(qs)
    acc[...] = jnp.zeros_like(acc)
    top[...] = jnp.zeros_like(top)
    stat[...] = jnp.zeros_like(stat)
    stat_last[...] = jnp.zeros_like(stat_last)

    def prepare(t):
        for ry, rz in TILES[t]:
            columns = pl.ds(QUERY_SLOT[ry, rz] * ROWS, ROWS)
            scaled = qb[ry, rz].astype(f32) * (LOG2E * HEAD_DIM**-0.5)
            high = scaled.astype(bf16)
            low = (scaled - high.astype(f32)).astype(bf16)
            for n, h, at_row in ((0, 0, 0), (1, 1, 1), (2, 2, 0), (3, 2, 1)):
                rows = slice(h * HEAD_DIM, (h + 1) * HEAD_DIM)
                qs[n, at_row * HEAD_DIM : (at_row + 1) * HEAD_DIM, columns] = high[rows]
                qs[n, ROWS + at_row * HEAD_DIM : ROWS + (at_row + 1) * HEAD_DIM, columns] = low[
                    rows
                ]

    for r in (1, 3, 2):
        queries_z(r).wait_recv()
        queries_y(1, r).start()
        queries_y(3, r).start()
    queries_y(1, 0).wait_recv()
    prepare(0)
    for r in (1, 3, 2):
        queries_y(2, r).start()

    def keys_in(copy, rx, rz):
        copy(rz).wait_recv()
        keys_core(rx, rz).start()

    def chunk_in(t):
        for rx, rz in CHUNKS[t]:
            keys_core(rx, rz).wait_recv()

    for r in (1, 3):
        keys_in(keys_z, 0, r)
        keys_up(r).start()
        keys_down(r).start()
    keys_z(2).start()
    keys_in(keys_up, 1, 0)
    keys_on(0).start()
    keys_in(keys_down, 3, 0)
    chunk_in(0)

    def tile(ry):
        return pl.ds(pl.multiple_of(ry * TILE, TILE), TILE)

    def score(g, h):
        chunk = 4 * lookup(CHUNK_AT, g)
        columns = tile(lookup(TILE_AT, g))
        rows = slice(0, ROWS) if h < 2 else slice(ROWS, KROWS)
        keys = jnp.concatenate(
            [kv[cc, chunk + n, rows, :] for cc in range(2) for n in range(4)], axis=0
        )
        keys = jnp.concatenate([keys, keys], axis=1)
        if h < 2:
            s = jnp.dot(keys, qs[h, :, columns], preferred_element_type=f32)
            sb[h] = s.reshape(8, 2, HEAD_DIM, TILE)
            most = jnp.max(s, axis=0, keepdims=True)
        else:
            sa = jnp.dot(keys, qs[2, :, columns], preferred_element_type=f32)
            sb[h, :, 0] = sa.reshape(8, HEAD_DIM, TILE)
            sc = jnp.dot(keys, qs[3, :, columns], preferred_element_type=f32)
            sb[h, :, 1] = sc.reshape(8, HEAD_DIM, TILE)
            most = jnp.maximum(
                jnp.max(sa, axis=0, keepdims=True), jnp.max(sc, axis=0, keepdims=True)
            )
        old = top[h, :, columns]
        new = jnp.maximum(old, most)
        shrink[h] = jnp.exp2(old - new)
        top[h, :, columns] = new
        cur[h] = new

    def weigh(g, h):
        chunk = 4 * lookup(CHUNK_AT, g)
        columns = tile(lookup(TILE_AT, g))
        chances = jnp.exp2(sb[h].reshape(8 * ROWS, TILE) - cur[h]).astype(bf16)
        first = KROWS + h * HEAD_DIM
        values = jnp.concatenate(
            [
                jnp.concatenate(
                    [
                        kv[cc, chunk + n, first : first + HEAD_DIM, :],
                        kv[cc, chunk + n, KROWS + GD :, :],
                    ],
                    axis=0,
                )
                for cc in range(2)
                for n in range(4)
            ],
            axis=1,
        )
        acc[h, :, columns] = acc[h, :, columns] * shrink[h] + jnp.dot(
            values, chances, preferred_element_type=f32
        )

    def step(g, between=None):
        score(g, 1)
        weigh(g, 0)
        score(g, 2)
        weigh(g, 1)
        if between is not None:
            between()
        score(g + 1, 0)
        weigh(g, 2)

    def pieces(store, at_row, value, n):
        for i in range(n):
            piece = value.astype(bf16).astype(f32)
            store[at_row(i), :] = piece
            value = value - piece

    def deliver(t):
        columns = pl.ds(t * TILE, TILE)
        for h in range(GH):
            pieces(stat, lambda i: pl.ds(GH * i + h, 1), top[h, :, columns], 3)
            total = acc[h, HEAD_DIM : HEAD_DIM + 1, columns]
            pieces(stat, lambda i: pl.ds(GH * (i + 3) + h, 1), total, 2)
        for n, (ry, rz) in enumerate(TILES[t]):
            slot = 4 * t + n
            for h in range(GH):
                rows = pl.ds(h * HEAD_DIM, HEAD_DIM)
                o_send[slot, rows, :] = acc[h, :HEAD_DIM, pl.ds(slot * ROWS, ROWS)].astype(bf16)
            o_send[slot, GD:, :] = stat[:, n * ROWS : (n + 1) * ROWS].astype(bf16)
            part(ry, rz).start()

    def deliver_last(h):
        columns = pl.ds(0, TILE)
        store = stat_last.at[h]
        pieces(store, lambda i: pl.ds(i, 1), top[h, :, columns], 3)
        pieces(store, lambda i: pl.ds(i + 3, 1), acc[h, HEAD_DIM : HEAD_DIM + 1, columns], 2)
        for n in (1, 2, 3, 0):
            to = h_send if n else h_recv
            to[n, h, :HEAD_DIM, :] = acc[h, :HEAD_DIM, pl.ds(n * ROWS, ROWS)].astype(bf16)
            to[n, h, HEAD_DIM:, :] = stat_last[h, :, n * ROWS : (n + 1) * ROWS].astype(bf16)
            if n:
                part_head(*TILES[0][n], h).start()

    def queries_in(t):
        for ry, rz in TILES[t]:
            if ry:
                queries_y(ry, rz).wait_recv()
        prepare(t)

    score(0, 0)
    step(0, lambda: queries_in(1))
    step(1, lambda: queries_in(3))
    keys_in(keys_z, 0, 2)
    keys_in(keys_down, 3, 1)
    keys_in(keys_up, 1, 1)
    keys_up(2).start()
    keys_down(2).start()
    keys_on(1).start()
    step(2, lambda: chunk_in(1))
    step(3)
    keys_in(keys_up, 1, 3)
    keys_on(3).start()
    keys_in(keys_down, 3, 3)
    step(4, lambda: queries_in(2))

    def loop(g, carry):
        @pl.when(g == 5)
        def _():
            keys_in(keys_down, 3, 2)
            keys_on(2).start()
            keys_in(keys_up, 1, 2)
            for rz in (0, 1):
                keys_in(keys_on, 2, rz)

        @pl.when(g == 6)
        def _():
            chunk_in(2)

        @pl.when(g == 7)
        def _():
            for rz in (3, 2):
                keys_in(keys_on, 2, rz)

        @pl.when(g == 8)
        def _():
            chunk_in(3)

        step(g)

        for n, t in ((9, 2), (10, 3), (12, 1)):

            @pl.when(g == n)
            def _():
                deliver(t)

        return carry

    lax.fori_loop(5, 15, loop, 0)
    score(15, 1)
    weigh(15, 0)
    score(15, 2)
    deliver_last(0)
    weigh(15, 1)
    deliver_last(1)
    weigh(15, 2)
    deliver_last(2)

    for t in (2, 3, 1):
        for ry, rz in TILES[t]:
            part(ry, rz).wait_recv()
    for h in range(GH):
        for ry, rz in TILES[0][1:]:
            part_head(ry, rz, h).wait_recv()
        for rz in range(4):
            row, weights = [], []
            for ry in range(4):
                n = QUERY_SLOT[ry, rz]
                if n < 4:
                    stats = h_recv[n, h, HEAD_DIM:, :].astype(f32)
                    row.append([stats[i : i + 1] for i in range(5)])
                    weights.append(h_recv[n, h, :HEAD_DIM, :])
                else:
                    stats = o_recv[n, GD:, :].astype(f32)
                    row.append([stats[GH * i + h : GH * i + h + 1] for i in range(5)])
                    weights.append(o_recv[n, h * HEAD_DIM : (h + 1) * HEAD_DIM, :])
            tops = [r[0] + r[1] + r[2] for r in row]
            most = jnp.maximum(jnp.maximum(tops[0], tops[1]), jnp.maximum(tops[2], tops[3]))
            total = jnp.exp2(-most)
            weighted = jnp.zeros((HEAD_DIM, ROWS), f32)
            for ry in range(4):
                factor = jnp.exp2(tops[ry] - most)
                total = total + (row[ry][3] + row[ry][4]) * factor
                weighted = weighted + weights[ry].astype(f32) * factor
            rows = slice(h * HEAD_DIM, (h + 1) * HEAD_DIM)
            out_ref[(z + rz) % 4, rows, :] = (weighted / total).astype(bf16)

    for r in (1, 2, 3):
        for copy in (queries_z, keys_z):
            copy(r).wait_send()
    for r in range(4):
        for copy in (keys_up, keys_down, keys_on):
            copy(r).wait_send()
        for rx in range(4):
            keys_core(rx, r).wait_send()
        for ry in (1, 2, 3):
            queries_y(ry, r).wait_send()
    for t in (1, 2, 3):
        for ry, rz in TILES[t]:
            part(ry, rz).wait_send()
    for h in range(GH):
        for ry, rz in TILES[0][1:]:
            part_head(ry, rz, h).wait_send()


def on_device(queries, keys, values, valid, out_weight):
    bf16, f32 = jnp.bfloat16, jnp.float32
    whole = pl.BlockSpec(memory_space=pltpu.VMEM)
    attended = pl.pallas_call(
        kernel,
        out_shape=jax.ShapeDtypeStruct((GROUPS, GD, ROWS), bf16),
        in_specs=[whole] * 4,
        out_specs=whole,
        scratch_shapes=[
            pltpu.VMEM((GROUPS, SHARD, ROWS), bf16),
            pltpu.VMEM((GROUPS, GD, ROWS), bf16),
            pltpu.VMEM((2, 16, SHARD, ROWS), bf16),
            pltpu.VMEM((4, 4, GD, ROWS), bf16),
            pltpu.VMEM((4, 2 * ROWS, 4 * TILE), bf16),
            pltpu.VMEM((GH, 8, 2, HEAD_DIM, TILE), f32),
            pltpu.VMEM((GH, HEAD_DIM + 16, 4 * TILE), f32),
            pltpu.VMEM((GH, 1, 4 * TILE), f32),
            pltpu.VMEM((GH, 1, TILE), f32),
            pltpu.VMEM((GH, 1, TILE), f32),
            pltpu.VMEM((16, TILE), f32),
            pltpu.VMEM((GH, 16, TILE), f32),
            pltpu.VMEM((16, PART, ROWS), bf16),
            pltpu.VMEM((16, PART, ROWS), bf16),
            pltpu.VMEM((4, GH, LAST, ROWS), bf16),
            pltpu.VMEM((4, GH, LAST, ROWS), bf16),
            pltpu.SemaphoreType.DMA((COPIES,)),
            pltpu.SemaphoreType.DMA((COPIES,)),
        ],
        compiler_params=pltpu.CompilerParams(
            collective_id=0, has_side_effects=True, vmem_limit_bytes=56 << 20
        ),
        name="attend",
    )(queries, keys, values, valid.reshape(1, ROWS))
    mixed = lax.dot_general(
        attended.reshape(HEADS * HEAD_DIM, ROWS),
        out_weight,
        (((0,), (0,)), ((), ())),
        preferred_element_type=f32,
    )
    return mixed.astype(bf16)


def solution(mesh):
    return jax.shard_map(
        on_device,
        mesh=mesh,
        in_specs=(
            P(("blk", "inner"), None),
            P(("blk", "inner"), None),
            P(("blk", "inner"), None),
            P(("blk", "inner")),
            P(),
        ),
        out_specs=P(("blk", "inner"), None),
        check_vma=False,
    )
```
